32 devices in a mesh: look: 16 (over z, y, core), swath: 2 (over x).
Axes of the slice: x: 2, y: 2, z: 4, core: 2. Of those that a mesh axis runs over, the one named last changes fastest.
Arguments:
- images: bfloat16 [32, 8, 2, 512, 512], P('look', 'swath'), may hold values from -6 to 6
- patch_weight: float32 [8], P('swath'), may hold values from 1 to 10
- pair_mask: int32 [32, 4], P('look'), may hold values 0 or 1
Outputs:
- drift: float32 [32, 4, 256, 256], P('look', None, 'swath')
The draws below stay inside these ranges and needn't reach their ends.
All inputs are finite; a program needn't handle non-finite values. No bound on the sum of `pair_mask` on one device may be relied on, other than what follows from the above.
Results may differ from the reference program's by a relative error of at most 0.015.
Values may be sent and summed in bfloat16 or wider, within the bound.
A program may use at most 128 MiB of HBM per device.

```python
import math
import jax
import jax.numpy as jnp
from jax import lax

PIX = 512
BAND = 256
WIN = 256
LAGS = 4
LOOKS = 32
PATCHES = 8


def place_ends(drawn, own_key, smallest, largest):
    longest = drawn.shape.index(max(drawn.shape))
    spots = []
    for shift in (0, 1):
        where = [jax.random.randint(jax.random.fold_in(own_key, axis), (), 0, length) for axis, length in enumerate(drawn.shape)]
        where[longest] = (where[longest] + shift) % drawn.shape[longest]
        spots.append(tuple(where))
    return drawn.at[spots[0]].set(smallest).at[spots[1]].set(largest)


def level_of(own_key, extent, cuts, least, high):
    loudness, own = 1.0, jax.random.fold_in(own_key, 6)
    for axis_at, shards_of in cuts:
        steps = jnp.exp(jax.random.uniform(jax.random.fold_in(own, axis_at), (shards_of,), jnp.float32, least / len(cuts), high / len(cuts)))
        loudness = loudness * jnp.repeat(steps, extent[axis_at] // shards_of).reshape([-1 if axis == axis_at else 1 for axis in range(len(extent))])
    return loudness


def centred(key, shape, spread, limit, pieces=(), kind=jnp.bfloat16):
    factor_of = level_of(key, shape, pieces, -0.22, 0.18) if pieces else 1.0
    drawn = jax.random.normal(key, shape, jnp.float32) * spread * factor_of
    return jnp.minimum(jnp.maximum(drawn, -limit), limit).astype(kind)


def setup_inputs(seed: int = 0) -> dict:
    key_list = jax.random.split(jax.random.key(seed), 4)
    images = centred(key_list[0], (LOOKS, PATCHES, 2, PIX, PIX), 1.0, 6.0, ((0, 16), (1, 2)))
    patch_weight = jnp.clip(jnp.exp(math.log(10.0) - 2.3025851 * jax.random.uniform(key_list[1], (PATCHES,), jnp.float32) ** level_of(key_list[1], (PATCHES,), ((0, 2),), -0.2, 0.2)), 1.0, 10.0)
    pair_mask = place_ends((jax.random.randint(key_list[2], (LOOKS, LAGS), 0, 4) < 3).astype(jnp.int32), jax.random.fold_in(key_list[2], 1), 0, 1)
    return dict(images=images, patch_weight=patch_weight, pair_mask=pair_mask)


def tables(rows, cols, row_shift, col_shift, sign):
    row_ids = jnp.arange(rows, dtype=jnp.int32) - row_shift
    col_ids = jnp.arange(cols, dtype=jnp.int32) - col_shift
    phase = row_ids[:, None] * col_ids[None, :] % PIX
    angle = 2.0 * math.pi / PIX * phase.astype(jnp.float32)
    return (jnp.cos(angle).astype(jnp.bfloat16), (sign * jnp.sin(angle)).astype(jnp.bfloat16))

def fdot(form, left, right):
    return jnp.einsum(form, left.astype(jnp.float32), right.astype(jnp.float32))

def spectra(block, fwd_re, fwd_im):
    img_re = block[:, 0]
    img_im = block[:, 1]
    rows_re = (fdot('kn,anm->akm', fwd_re, img_re) - fdot('kn,anm->akm', fwd_im, img_im)).astype(jnp.bfloat16)
    rows_im = (fdot('kn,anm->akm', fwd_re, img_im) + fdot('kn,anm->akm', fwd_im, img_re)).astype(jnp.bfloat16)
    spec_re = (fdot('akm,lm->akl', rows_re, fwd_re) - fdot('akm,lm->akl', rows_im, fwd_im)).astype(jnp.bfloat16)
    spec_im = (fdot('akm,lm->akl', rows_re, fwd_im) + fdot('akm,lm->akl', rows_im, fwd_re)).astype(jnp.bfloat16)
    return jnp.stack([spec_re, spec_im], axis=1)

def surface_of(own, partner, weights, inv_re, inv_im):
    own_re = own[:, 0].astype(jnp.float32)
    own_im = own[:, 1].astype(jnp.float32)
    par_re = partner[:, 0].astype(jnp.float32)
    par_im = partner[:, 1].astype(jnp.float32)
    cross_re = (own_re * par_re + own_im * par_im).astype(jnp.bfloat16)
    cross_im = (own_im * par_re - own_re * par_im).astype(jnp.bfloat16)
    shift_re = (fdot('tf,pfg->ptg', inv_re, cross_re) - fdot('tf,pfg->ptg', inv_im, cross_im)).astype(jnp.bfloat16)
    shift_im = (fdot('tf,pfg->ptg', inv_re, cross_im) + fdot('tf,pfg->ptg', inv_im, cross_re)).astype(jnp.bfloat16)
    real_part = fdot('ptg,ug->ptu', shift_re, inv_re) - fdot('ptg,ug->ptu', shift_im, inv_im)
    return jnp.einsum('p,ptu->tu', weights, real_part)

def reference(images, patch_weight, pair_mask):
    fwd_re, fwd_im = tables(BAND, PIX, BAND // 2, 0, -1.0)
    inv_re, inv_im = tables(WIN, BAND, WIN // 2, BAND // 2, 1.0)
    spectrum = lax.map(lambda block: spectra(block, fwd_re, fwd_im), images)

    def energy_of(spec):
        sq = spec.astype(jnp.float32)
        return jnp.sum(patch_weight * lax.optimization_barrier(jnp.sum(sq * sq, axis=(1, 2, 3))))
    energy = lax.map(energy_of, spectrum)
    scale = BAND * math.sqrt(PATCHES)

    def one_look(look):
        own = lax.dynamic_index_in_dim(spectrum, look, 0, keepdims=False)
        outs = []
        for offset in (1, 2, 3, LOOKS // 2):
            mate = ((look + offset) % LOOKS).astype(jnp.int32)
            partner = lax.dynamic_index_in_dim(spectrum, mate, 0, keepdims=False)
            surf = surface_of(own, partner, patch_weight, inv_re, inv_im)
            denom = jnp.sqrt(energy[look] * energy[mate])
            outs.append(surf * scale / denom)
        return jnp.stack(outs, axis=0)
    surfaces = lax.map(one_look, jnp.arange(LOOKS, dtype=jnp.int32))
    return surfaces * pair_mask.astype(jnp.float32)[:, :, None, None]
```

```python
import functools
import math

import jax
import jax.numpy as jnp
import numpy as np
from jax import lax
from jax.experimental import pallas as pl
from jax.experimental.pallas import tpu as pltpu
from jax.sharding import PartitionSpec as P

PIX = 512
BAND = 256
WIN = 256
HALF = PIX // 2


def phases(rows, cols, row_shift, col_shift):
    phase = (rows[:, None] - row_shift) * (cols[None, :] - col_shift) % PIX
    angle = 2.0 * math.pi / PIX * phase
    return np.cos(angle), np.sin(angle)


def forward_tables():
    left, right = [], []
    for parity in (0, 1):
        re, im = phases(np.arange(parity, BAND, 2), np.arange(HALF), BAND // 2, 0)
        im = -im
        left.append(np.block([[re, -im], [im, re]]))
        right.append(np.block([[re.T, im.T], [-im.T, re.T]]))
    return jnp.asarray(np.stack(left), jnp.bfloat16), jnp.asarray(np.stack(right), jnp.bfloat16)


def inverse_tables():
    order = np.concatenate([np.arange(0, BAND, 2), np.arange(1, BAND, 2)])
    re, im = phases(np.arange(WIN), order, WIN // 2, BAND // 2)
    first = np.concatenate([re, im], axis=0)
    second = np.stack([re.T, im.T])
    return jnp.asarray(first, jnp.bfloat16), jnp.asarray(second, jnp.bfloat16)


def dot(left, right):
    return jnp.dot(left, right, preferred_element_type=jnp.float32)


def spectrum_kernel(img_ref, left_ref, right_ref, spec_ref, energy_ref):
    re0, re1 = img_ref[0, 0, :HALF, :], img_ref[0, 0, HALF:, :]
    im0, im1 = img_ref[0, 1, :HALF, :], img_ref[0, 1, HALF:, :]
    even = dot(left_ref[0], jnp.concatenate([re0 + re1, im0 + im1], axis=0))
    odd = dot(left_ref[1], jnp.concatenate([re0 - re1, im0 - im1], axis=0))
    quarter = BAND // 2
    parts = []
    for at in (0, quarter):
        parts.append(jnp.concatenate([even[at : at + quarter], odd[at : at + quarter]], axis=0))
    plus = [(part[:, :HALF] + part[:, HALF:]).astype(jnp.bfloat16) for part in parts]
    minus = [(part[:, :HALF] - part[:, HALF:]).astype(jnp.bfloat16) for part in parts]
    spec_even = dot(jnp.concatenate(plus, axis=1), right_ref[0]).astype(jnp.bfloat16)
    spec_odd = dot(jnp.concatenate(minus, axis=1), right_ref[1]).astype(jnp.bfloat16)
    spec_ref[0, 0, :, :quarter] = spec_even[:, :quarter]
    spec_ref[0, 0, :, quarter:] = spec_odd[:, :quarter]
    spec_ref[0, 1, :, :quarter] = spec_even[:, quarter:]
    spec_ref[0, 1, :, quarter:] = spec_odd[:, quarter:]
    total = spec_even.astype(jnp.float32) ** 2 + spec_odd.astype(jnp.float32) ** 2
    folded = jnp.sum(total.reshape(BAND // 8, 8, BAND), axis=0)
    energy_ref[0] = folded[:, :quarter] + folded[:, quarter:]


def spectra(images, left, right):
    looks, patches = images.shape[:2]
    flat = images.reshape((looks * patches,) + images.shape[2:])
    count = flat.shape[0]
    spec, energy = pl.pallas_call(
        spectrum_kernel,
        grid=(count,),
        in_specs=[
            pl.BlockSpec((1, 2, PIX, PIX), lambda i: (i, 0, 0, 0)),
            pl.BlockSpec(left.shape, lambda i: (0, 0, 0)),
            pl.BlockSpec(right.shape, lambda i: (0, 0, 0)),
        ],
        out_specs=[
            pl.BlockSpec((1, 2, BAND, BAND), lambda i: (i, 0, 0, 0)),
            pl.BlockSpec((1, 8, 128), lambda i: (i, 0, 0)),
        ],
        out_shape=[
            jax.ShapeDtypeStruct((count, 2, BAND, BAND), jnp.bfloat16),
            jax.ShapeDtypeStruct((count, 8, 128), jnp.float32),
        ],
        name="spectra",
    )(flat, left, right)
    return spec.reshape(looks, patches, 2, BAND, BAND), energy.reshape(looks, patches, 8, 128)


ROWS = 32


def cross_into(w_ref, a_ref, a, b_ref, b, cre, cim):
    patches = a_ref.shape[1]

    def step(i, carry):
        rows = pl.ds(pl.multiple_of(i * ROWS, ROWS), ROWS)
        re = jnp.zeros((ROWS, BAND), jnp.float32)
        im = jnp.zeros((ROWS, BAND), jnp.float32)
        for p in range(patches):
            weight = w_ref[p]
            ar = a_ref[a, p, 0, rows, :].astype(jnp.float32) * weight
            ai = a_ref[a, p, 1, rows, :].astype(jnp.float32) * weight
            br = b_ref[b, p, 0, rows, :].astype(jnp.float32)
            bi = b_ref[b, p, 1, rows, :].astype(jnp.float32)
            re += ar * br + ai * bi
            im += ai * br - ar * bi
        cre[rows, :] = re.astype(jnp.bfloat16)
        cim[rows, :] = im.astype(jnp.bfloat16)
        return carry

    lax.fori_loop(0, BAND // ROWS, step, 0)


def halves(first_ref, second_ref, cre, cim):
    from_re = dot(first_ref[...], cre[...]).astype(jnp.bfloat16)
    from_im = dot(first_ref[...], cim[...]).astype(jnp.bfloat16)
    keep = dot(from_re[:WIN], second_ref[0]) - dot(from_re[WIN:], second_ref[1])
    turn = dot(from_im[:WIN], second_ref[1]) + dot(from_im[WIN:], second_ref[0])
    return keep, turn


def near_kernel(w_ref, own_ref, near0_ref, near1_ref, first_ref, second_ref, out_ref, cre, cim):
    pairs = ((0, own_ref, 1), (0, near0_ref, 0), (0, near1_ref, 0), (1, near0_ref, 0), (1, near1_ref, 0))
    for slot, (a, b_ref, b) in enumerate(pairs):
        cross_into(w_ref, own_ref, a, b_ref, b, cre, cim)
        keep, turn = halves(first_ref, second_ref, cre, cim)
        out_ref[slot] = keep - turn


def last_kernel(w_ref, own_ref, kept_ref, far_ref, opp_ref, first_ref, second_ref, out_ref, cre, cim):
    cross_into(w_ref, own_ref, 1, far_ref, 0, cre, cim)
    keep, turn = halves(first_ref, second_ref, cre, cim)
    out_ref[0] = keep - turn
    cross_into(w_ref, kept_ref, 0, opp_ref, 0, cre, cim)
    keep, turn = halves(first_ref, second_ref, cre, cim)
    out_ref[1] = keep - turn
    out_ref[2] = keep + turn


def pair_call(kernel, surfaces, weights, *operands):
    vmem = pl.BlockSpec(memory_space=pltpu.VMEM)
    return pl.pallas_call(
        kernel,
        in_specs=[pl.BlockSpec(memory_space=pltpu.SMEM)] + [vmem] * len(operands),
        out_specs=vmem,
        out_shape=jax.ShapeDtypeStruct((surfaces, WIN, WIN), jnp.float32),
        scratch_shapes=[pltpu.VMEM((BAND, BAND), jnp.bfloat16)] * 2,
        cost_estimate=pl.CostEstimate(
            flops=surfaces * 3 * 10**8, bytes_accessed=6 * 2**20, transcendentals=0
        ),
        name="pairs",
    )(weights, *operands)


def from_ahead(array, by):
    devices = lax.axis_size("look")
    return lax.ppermute(array, "look", [(i, (i - by) % devices) for i in range(devices)])


def exchange(array, look_by, swath_by):
    looks, swaths = lax.axis_size("look"), lax.axis_size("swath")
    pairs = []
    for i in range(looks):
        for j in range(swaths):
            to = (i + look_by) % looks * swaths + (j + swath_by) % swaths
            pairs.append((i * swaths + j, to))
    return lax.ppermute(array, ("look", "swath"), pairs)


def per_device(images, patch_weight, pair_mask):
    nlook = lax.axis_size("look")
    nswath = lax.axis_size("swath")
    me_swath = lax.axis_index("swath")
    low = lax.axis_index("look") < nlook // 2
    left, right = forward_tables()
    first, second = inverse_tables()
    own, squares = spectra(images, left, right)

    near0 = from_ahead(own[:1], 1)
    kept = jnp.where(low, own[:1], own[1:])
    opp = from_ahead(jnp.where(low, own[1:], own[:1]), nlook // 2)
    near1 = from_ahead(own[1:], 1)
    far = from_ahead(near0, 1)

    energy = jnp.einsum("p,lp->l", patch_weight, jnp.sum(squares, axis=(2, 3)))
    energy = energy + sum(exchange(energy, 0, by) for by in range(1, nswath))
    energy_near = from_ahead(energy, 1)
    energy_far = from_ahead(energy, 2)
    energy_opp = from_ahead(energy, nlook // 2)
    ring = jnp.concatenate([energy, energy_near, energy_far])
    mates = jnp.stack(
        [jnp.stack([ring[look + 1], ring[look + 2], ring[look + 3], energy_opp[look]]) for look in (0, 1)]
    )
    scale = BAND * math.sqrt(patch_weight.shape[0] * nswath)
    factor = pair_mask.astype(jnp.float32) * scale / jnp.sqrt(energy[:, None] * mates)

    surf_near = pair_call(near_kernel, 5, patch_weight, own, near0, near1, first, second)
    surf_last = pair_call(last_kernel, 3, patch_weight, own, kept, far, opp, first, second)

    rows = WIN // nswath

    def cut(array, by):
        return lax.dynamic_slice_in_dim(array, (me_swath + by) % nswath * rows, rows, axis=1)

    near_sum = cut(surf_near, 0)
    last_sum = cut(surf_last[:2], 0)
    back = exchange(cut(surf_last[2:], 0).astype(jnp.bfloat16), nlook // 2, 0).astype(jnp.float32)
    for by in range(1, nswath):
        near_sum += exchange(cut(surf_near, by).astype(jnp.bfloat16), 0, by).astype(jnp.float32)
        last_sum += exchange(cut(surf_last[:2], by).astype(jnp.bfloat16), 0, by).astype(jnp.float32)
        back += exchange(cut(surf_last[2:], by).astype(jnp.bfloat16), nlook // 2, by).astype(jnp.float32)
    opp_own = last_sum[1]
    surf0 = [near_sum[0], near_sum[1], near_sum[2], jnp.where(low, opp_own, back[0])]
    surf1 = [near_sum[3], near_sum[4], last_sum[0], jnp.where(low, back[0], opp_own)]
    return jnp.stack([jnp.stack(surf0), jnp.stack(surf1)]) * factor[:, :, None, None]


def solution(mesh):
    return jax.shard_map(
        per_device,
        mesh=mesh,
        in_specs=(P("look", "swath", None, None, None), P("swath"), P("look", None)),
        out_specs=P("look", None, "swath", None),
        check_vma=False,
    )
```

```python
import functools
import math

import jax
import jax.numpy as jnp
import numpy as np
from jax import lax
from jax.experimental import pallas as pl
from jax.experimental.pallas import tpu as pltpu
from jax.sharding import PartitionSpec as P

PIX = 512
BAND = 256
WIN = 256
HALF = PIX // 2


def phases(rows, cols, row_shift, col_shift):
    phase = (rows[:, None] - row_shift) * (cols[None, :] - col_shift) % PIX
    angle = 2.0 * math.pi / PIX * phase
    return np.cos(angle), np.sin(angle)


def forward_tables():
    left, right = [], []
    for parity in (0, 1):
        re, im = phases(np.arange(parity, BAND, 2), np.arange(HALF), BAND // 2, 0)
        im = -im
        left.append(np.block([[re, -im], [im, re]]))
        right.append(np.block([[re.T, im.T], [-im.T, re.T]]))
    return jnp.asarray(np.stack(left), jnp.bfloat16), jnp.asarray(np.stack(right), jnp.bfloat16)


def inverse_tables():
    order = np.concatenate([np.arange(0, BAND, 2), np.arange(1, BAND, 2)])
    re, im = phases(np.arange(WIN), order, WIN // 2, BAND // 2)
    first = np.concatenate([re, im], axis=0)
    second = np.stack([re.T, im.T])
    return jnp.asarray(first, jnp.bfloat16), jnp.asarray(second, jnp.bfloat16)


def dot(left, right):
    return jnp.dot(left, right, preferred_element_type=jnp.float32)


ROWS = 32
MESH = pl.DeviceIdType.MESH


def spectrum_of(img, left_ref, right_ref):
    re0, re1 = img[0, :HALF, :], img[0, HALF:, :]
    im0, im1 = img[1, :HALF, :], img[1, HALF:, :]
    even = dot(left_ref[0], jnp.concatenate([re0 + re1, im0 + im1], axis=0))
    odd = dot(left_ref[1], jnp.concatenate([re0 - re1, im0 - im1], axis=0))
    quarter = BAND // 2
    parts = []
    for at in (0, quarter):
        parts.append(jnp.concatenate([even[at : at + quarter], odd[at : at + quarter]], axis=0))
    plus = [(part[:, :HALF] + part[:, HALF:]).astype(jnp.bfloat16) for part in parts]
    minus = [(part[:, :HALF] - part[:, HALF:]).astype(jnp.bfloat16) for part in parts]
    spec_even = dot(jnp.concatenate(plus, axis=1), right_ref[0]).astype(jnp.bfloat16)
    spec_odd = dot(jnp.concatenate(minus, axis=1), right_ref[1]).astype(jnp.bfloat16)
    return spec_even, spec_odd


def squares_of(spec_even, spec_odd):
    total = spec_even.astype(jnp.float32) ** 2 + spec_odd.astype(jnp.float32) ** 2
    folded = jnp.sum(total.reshape(BAND // 8, 8, BAND), axis=0)
    return folded[:, : BAND // 2] + folded[:, BAND // 2 :]


def cross_into(w_ref, a_ref, b_ref, cre, cim):
    patches = a_ref.shape[0]

    def step(i, carry):
        rows = pl.ds(pl.multiple_of(i * ROWS, ROWS), ROWS)
        re = jnp.zeros((ROWS, BAND), jnp.float32)
        im = jnp.zeros((ROWS, BAND), jnp.float32)
        for p in range(patches):
            weight = w_ref[p]
            ar = a_ref[p, 0, rows, :].astype(jnp.float32) * weight
            ai = a_ref[p, 1, rows, :].astype(jnp.float32) * weight
            br = b_ref[p, 0, rows, :].astype(jnp.float32)
            bi = b_ref[p, 1, rows, :].astype(jnp.float32)
            re += ar * br + ai * bi
            im += ai * br - ar * bi
        cre[rows, :] = re.astype(jnp.bfloat16)
        cim[rows, :] = im.astype(jnp.bfloat16)
        return carry

    lax.fori_loop(0, BAND // ROWS, step, 0)


def halves(first_ref, second_ref, cre, cim):
    from_re = dot(first_ref[...], cre[...]).astype(jnp.bfloat16)
    from_im = dot(first_ref[...], cim[...]).astype(jnp.bfloat16)
    keep = dot(from_re[:WIN], second_ref[0]) - dot(from_re[WIN:], second_ref[1])
    turn = dot(from_im[:WIN], second_ref[1]) + dot(from_im[WIN:], second_ref[0])
    return keep, turn


PAIRS = 7


def kernel(nlook, nswath, w_ref, mask_ref, img_ref, left_ref, right_ref, first_ref, second_ref, out_ref,
           img, own, near, far, opp, energy, heard, cre, cim, surf, outbox, inbox, backbox,
           img_sem, near_send, near_recv, far_send, far_recv, opp_send, opp_recv,
           heard_send, heard_recv, box_send, box_recv, back_send, back_recv):
    looks, patches = img_ref.shape[:2]
    half = nlook // 2
    me, lane = lax.axis_index("look"), lax.axis_index("swath")
    odd = lax.rem(me, 2) == 1
    low = me < half
    sent_look = jnp.where(low, 1, 0)
    kept_look = 1 - sent_look

    def device(look_by, swath_by=0):
        return (lax.rem(me + look_by + nlook, nlook), lax.rem(lane + swath_by, nswath))

    def load(u):
        return pltpu.make_async_copy(img_ref.at[u // patches, u % patches], img.at[u], img_sem.at[u])

    for u in range(looks * patches):
        load(u).start()

    barrier = pltpu.get_barrier_semaphore()
    greeted = 0
    for look_by in (0, 1, -1, 2, -2, half):
        for by in range(nswath):
            if look_by or by:
                greeted += 1
                pl.semaphore_signal(barrier, inc=1, device_id=device(look_by, by), device_id_type=MESH)
    pl.semaphore_wait(barrier, greeted)

    def remote(src, dst, send, recv, to):
        return pltpu.make_async_remote_copy(
            src_ref=src, dst_ref=dst, send_sem=send, recv_sem=recv, device_id=to, device_id_type=MESH
        )

    def to_near(look, p):
        at = look * patches + p
        return remote(own.at[look, p], near.at[look, p], near_send.at[at], near_recv.at[at], device(-1))

    def to_opp(p):
        return remote(own.at[sent_look, p], opp.at[p], opp_send.at[p], opp_recv.at[p], device(half))

    def to_far(p):
        return remote(own.at[0, p], far.at[p], far_send.at[p], far_recv.at[p], device(-2))

    def relay(p):
        sem = far_send.at[patches + p]
        return remote(near.at[0, p], far.at[p], sem, far_recv.at[p], device(-1))

    def send(look, p):
        to_near(look, p).start()

        @pl.when(jnp.logical_and(odd, look == 0))
        def _():
            to_far(p).start()

        @pl.when(look == sent_look)
        def _():
            to_opp(p).start()

    for look in range(looks):
        energy[look] = jnp.zeros((8, 128), jnp.float32)

    def forward(u, carry):
        look, p = u // patches, u % patches
        load_u = pltpu.make_async_copy(img_ref.at[look, p], img.at[u], img_sem.at[u])
        load_u.wait()
        spec_even, spec_odd = spectrum_of(img.at[u], left_ref, right_ref)
        quarter = BAND // 2
        own[look, p, 0, :, :quarter] = spec_even[:, :quarter]
        own[look, p, 0, :, quarter:] = spec_odd[:, :quarter]
        own[look, p, 1, :, :quarter] = spec_even[:, quarter:]
        own[look, p, 1, :, quarter:] = spec_odd[:, quarter:]
        energy[look] += w_ref[p] * squares_of(spec_even, spec_odd)

        @pl.when(u > 0)
        def _():
            send((u - 1) // patches, (u - 1) % patches)

        return carry

    lax.fori_loop(0, looks * patches, forward, 0)
    send(looks - 1, patches - 1)

    tell = []
    for d, look_by in enumerate((0, 1, 2, half)):
        for by in range(nswath):
            if look_by or by:
                tell.append(remote(energy, heard.at[d, by], heard_send.at[d, by], heard_recv.at[d, by],
                                   device(-look_by, by)))
    for copy in tell:
        copy.start()

    rows = WIN // nswath
    mine = pl.ds(pl.multiple_of(lane * rows, rows), rows)

    def outgoing(slot, by):
        at = pl.ds(pl.multiple_of(lax.rem(lane + by, nswath) * rows, rows), rows)
        return remote(outbox.at[slot, at], inbox.at[by - 1, slot], box_send.at[by - 1, slot],
                      box_recv.at[by - 1, slot], device(0, by))

    def returned(by):
        at = pl.ds(pl.multiple_of(lax.rem(lane + by, nswath) * rows, rows), rows)
        return remote(outbox.at[PAIRS, at], backbox.at[by], back_send.at[by], back_recv.at[by],
                      device(half, by))

    def pair(slot, a, b_ref):
        cross_into(w_ref, own.at[a], b_ref, cre, cim)
        keep, turn = halves(first_ref, second_ref, cre, cim)
        value = keep - turn
        surf[slot] = value
        outbox[slot] = value.astype(jnp.bfloat16)
        if slot == PAIRS - 1:
            outbox[PAIRS] = (keep + turn).astype(jnp.bfloat16)
            for by in range(nswath):
                returned(by).start()
        for by in range(1, nswath):
            outgoing(slot, by).start()

    pair(0, 0, own.at[1])
    for p in range(patches):
        to_near(0, p).wait_recv()

        @pl.when(odd)
        def _():
            relay(p).start()

    pair(1, 0, near.at[0])
    pair(3, 1, near.at[0])
    for p in range(patches):
        to_near(1, p).wait_recv()
    pair(2, 0, near.at[1])
    pair(4, 1, near.at[1])
    for p in range(patches):
        to_far(p).wait_recv()
    pair(5, 1, far)
    for p in range(patches):
        to_opp(p).wait_recv()
    pair(6, kept_look, opp)

    for copy in tell:
        copy.wait_recv()
    total = []
    for d in range(4):
        for look in range(looks):
            parts = energy[look] if d == 0 else heard[d, 0, look]
            for by in range(1, nswath):
                parts = parts + heard[d, by, look]
            total.append(jnp.sum(parts, axis=(0, 1), keepdims=True))
    scale = BAND * math.sqrt(patches * nswath)

    def factor(look, lag):
        mate = total[look + lag + 1] if lag < 3 else total[3 * looks + look]
        return mask_ref[look, lag].astype(jnp.float32) * scale / jnp.sqrt(total[look] * mate)

    def summed(slot):
        value = surf[slot, mine, :]
        for by in range(1, nswath):
            outgoing(slot, by).wait_recv()
            value = value + inbox[by - 1, slot].astype(jnp.float32)
        return value

    for slot in range(PAIRS - 1):
        out_ref[slot // 3, slot % 3] = summed(slot) * factor(slot // 3, slot % 3)
    kept = summed(PAIRS - 1)
    back = jnp.zeros((rows, WIN), jnp.float32)
    for by in range(nswath):
        returned(by).wait_recv()
        back = back + backbox[by].astype(jnp.float32)
    out_ref[0, 3] = jnp.where(low, kept, back) * factor(0, 3)
    out_ref[1, 3] = jnp.where(low, back, kept) * factor(1, 3)

    for look in range(looks):
        for p in range(patches):
            to_near(look, p).wait_send()
    for p in range(patches):
        to_opp(p).wait_send()

        @pl.when(odd)
        def _():
            to_far(p).wait_send()
            relay(p).wait_send()

    for copy in tell:
        copy.wait_send()
    for by in range(nswath):
        returned(by).wait_send()
    for slot in range(PAIRS):
        for by in range(1, nswath):
            outgoing(slot, by).wait_send()


def per_device(images, patch_weight, pair_mask):
    nlook = lax.axis_size("look")
    nswath = lax.axis_size("swath")
    looks, patches = images.shape[:2]
    left, right = forward_tables()
    first, second = inverse_tables()
    rows = WIN // nswath
    vmem = pl.BlockSpec(memory_space=pltpu.VMEM)
    smem = pl.BlockSpec(memory_space=pltpu.SMEM)
    dma = pltpu.SemaphoreType.DMA
    unit = (2, BAND, BAND)
    others = max(nswath - 1, 1)
    return pl.pallas_call(
        functools.partial(kernel, nlook, nswath),
        in_specs=[smem, smem, pl.BlockSpec(memory_space=pl.ANY)] + [vmem] * 4,
        out_specs=vmem,
        out_shape=jax.ShapeDtypeStruct((looks, 4, rows, WIN), jnp.float32),
        scratch_shapes=[
            pltpu.VMEM((looks * patches, 2, PIX, PIX), jnp.bfloat16),
            pltpu.VMEM((looks, patches) + unit, jnp.bfloat16),
            pltpu.VMEM((looks, patches) + unit, jnp.bfloat16),
            pltpu.VMEM((patches,) + unit, jnp.bfloat16),
            pltpu.VMEM((patches,) + unit, jnp.bfloat16),
            pltpu.VMEM((looks, 8, 128), jnp.float32),
            pltpu.VMEM((4, nswath, looks, 8, 128), jnp.float32),
            pltpu.VMEM((BAND, BAND), jnp.bfloat16),
            pltpu.VMEM((BAND, BAND), jnp.bfloat16),
            pltpu.VMEM((PAIRS, WIN, WIN), jnp.float32),
            pltpu.VMEM((PAIRS + 1, WIN, WIN), jnp.bfloat16),
            pltpu.VMEM((others, PAIRS, rows, WIN), jnp.bfloat16),
            pltpu.VMEM((nswath, rows, WIN), jnp.bfloat16),
            dma((looks * patches,)),
            dma((looks * patches,)),
            dma((looks * patches,)),
            dma((2 * patches,)),
            dma((patches,)),
            dma((patches,)),
            dma((patches,)),
            dma((4, nswath)),
            dma((4, nswath)),
            dma((others, PAIRS)),
            dma((others, PAIRS)),
            dma((nswath,)),
            dma((nswath,)),
        ],
        compiler_params=pltpu.CompilerParams(
            collective_id=0, has_side_effects=True, vmem_limit_bytes=48 * 2**20
        ),
        name="autofocus",
    )(patch_weight, pair_mask, images, left, right, first, second)


def solution(mesh):
    return jax.shard_map(
        per_device,
        mesh=mesh,
        in_specs=(P("look", "swath", None, None, None), P("swath"), P("look", None)),
        out_specs=P("look", None, "swath", None),
        check_vma=False,
    )
```

```python
import functools
import math

import jax
import jax.numpy as jnp
import numpy as np
from jax import lax
from jax.experimental import pallas as pl
from jax.experimental.pallas import tpu as pltpu
from jax.sharding import PartitionSpec as P

PIX = 512
BAND = 256
WIN = 256
HALF = PIX // 2


def phases(rows, cols, row_shift, col_shift):
    phase = (rows[:, None] - row_shift) * (cols[None, :] - col_shift) % PIX
    angle = 2.0 * math.pi / PIX * phase
    return np.cos(angle), np.sin(angle)


def forward_tables():
    left, right = [], []
    for parity in (0, 1):
        re, im = phases(np.arange(parity, BAND, 2), np.arange(HALF), BAND // 2, 0)
        im = -im
        left.append(np.block([[re, -im], [im, re]]))
        right.append(np.block([[re.T, im.T], [-im.T, re.T]]))
    return jnp.asarray(np.stack(left), jnp.bfloat16), jnp.asarray(np.stack(right), jnp.bfloat16)


def inverse_tables():
    order = np.concatenate([np.arange(0, BAND, 2), np.arange(1, BAND, 2)])
    re, im = phases(np.arange(WIN), order, WIN // 2, BAND // 2)
    first = np.concatenate([re, im], axis=0)
    second = np.stack([re.T, im.T])
    return jnp.asarray(first, jnp.bfloat16), jnp.asarray(second, jnp.bfloat16)


def dot(left, right):
    return jnp.dot(left, right, preferred_element_type=jnp.float32)


ROWS = 32
MESH = pl.DeviceIdType.MESH


def spectrum_of(img, left_ref, right_ref):
    re0, re1 = img[0, :HALF, :], img[0, HALF:, :]
    im0, im1 = img[1, :HALF, :], img[1, HALF:, :]
    even = dot(left_ref[0], jnp.concatenate([re0 + re1, im0 + im1], axis=0))
    odd = dot(left_ref[1], jnp.concatenate([re0 - re1, im0 - im1], axis=0))
    quarter = BAND // 2
    parts = []
    for at in (0, quarter):
        parts.append(jnp.concatenate([even[at : at + quarter], odd[at : at + quarter]], axis=0))
    plus = [(part[:, :HALF] + part[:, HALF:]).astype(jnp.bfloat16) for part in parts]
    minus = [(part[:, :HALF] - part[:, HALF:]).astype(jnp.bfloat16) for part in parts]
    spec_even = dot(jnp.concatenate(plus, axis=1), right_ref[0]).astype(jnp.bfloat16)
    spec_odd = dot(jnp.concatenate(minus, axis=1), right_ref[1]).astype(jnp.bfloat16)
    return spec_even, spec_odd


def squares_of(spec_even, spec_odd):
    total = spec_even.astype(jnp.float32) ** 2 + spec_odd.astype(jnp.float32) ** 2
    folded = jnp.sum(total.reshape(BAND // 8, 8, BAND), axis=0)
    return folded[:, : BAND // 2] + folded[:, BAND // 2 :]


def cross_into(w_ref, a_ref, b_ref, cre, cim):
    patches = a_ref.shape[0]

    def step(i, carry):
        rows = pl.ds(pl.multiple_of(i * ROWS, ROWS), ROWS)
        re = jnp.zeros((ROWS, BAND), jnp.float32)
        im = jnp.zeros((ROWS, BAND), jnp.float32)
        for p in range(patches):
            weight = w_ref[p]
            ar = a_ref[p, 0, rows, :].astype(jnp.float32) * weight
            ai = a_ref[p, 1, rows, :].astype(jnp.float32) * weight
            br = b_ref[p, 0, rows, :].astype(jnp.float32)
            bi = b_ref[p, 1, rows, :].astype(jnp.float32)
            re += ar * br + ai * bi
            im += ai * br - ar * bi
        cre[rows, :] = re.astype(jnp.bfloat16)
        cim[rows, :] = im.astype(jnp.bfloat16)
        return carry

    lax.fori_loop(0, BAND // ROWS, step, 0)


def halves(first_ref, second_ref, cre, cim):
    from_re = dot(first_ref[...], cre[...]).astype(jnp.bfloat16)
    from_im = dot(first_ref[...], cim[...]).astype(jnp.bfloat16)
    keep = dot(from_re[:WIN], second_ref[0]) - dot(from_re[WIN:], second_ref[1])
    turn = dot(from_im[:WIN], second_ref[1]) + dot(from_im[WIN:], second_ref[0])
    return keep, turn


PAIRS = 7


def kernel(nlook, nswath, w_ref, mask_ref, img_ref, left_hbm, right_hbm, first_hbm, second_hbm, out_ref,
           left_ref, right_ref, first_ref, second_ref, img, hop, own, near, far, opp, energy, heard, cre, cim, surf, outbox, inbox, backbox,
           table_sem, hop_send, hop_recv, onward_send, img_sem, near_send, near_recv, far_send, far_recv, opp_send, opp_recv,
           heard_send, heard_recv, box_send, box_recv, back_send, back_recv):
    looks, patches = img_ref.shape[:2]
    half = nlook // 2
    me, lane = lax.axis_index("look"), lax.axis_index("swath")
    odd = lax.rem(me, 2) == 1
    crossing = lax.rem(me, 4) < 2
    low = me < half
    sent_look = jnp.where(low, 1, 0)
    kept_look = 1 - sent_look

    def device(look_by, swath_by=0):
        return (lax.rem(me + look_by + nlook, nlook), lax.rem(lane + swath_by, nswath))

    def load(u):
        return pltpu.make_async_copy(img_ref.at[u // patches, u % patches], img.at[u], img_sem.at[u])

    tables = [
        pltpu.make_async_copy(src, dst, table_sem.at[i])
        for i, (src, dst) in enumerate(
            ((left_hbm, left_ref), (right_hbm, right_ref), (first_hbm, first_ref), (second_hbm, second_ref))
        )
    ]
    load(0).start()
    tables[0].start()
    tables[1].start()
    for u in range(1, looks * patches):
        load(u).start()
    tables[2].start()
    tables[3].start()

    barrier = pltpu.get_barrier_semaphore()
    greeted = 0
    for look_by in (0, 1, -1, 2, -2, half):
        for by in range(nswath):
            if look_by or by:
                greeted += 1
                pl.semaphore_signal(barrier, inc=1, device_id=device(look_by, by), device_id_type=MESH)
    for look_by in (3, -3, 4, -4):
        greeted += 1
        pl.semaphore_signal(barrier, inc=1, device_id=device(look_by), device_id_type=MESH)
    pl.semaphore_wait(barrier, greeted)

    def remote(src, dst, send, recv, to):
        return pltpu.make_async_remote_copy(
            src_ref=src, dst_ref=dst, send_sem=send, recv_sem=recv, device_id=to, device_id_type=MESH
        )

    def to_near(look, p):
        at = look * patches + p
        return remote(own.at[look, p], near.at[look, p], near_send.at[at], near_recv.at[at], device(-1))

    def to_opp(p):
        return remote(own.at[sent_look, p], opp.at[p], opp_send.at[p], opp_recv.at[p], device(half))

    def to_far(p):
        return remote(own.at[0, p], far.at[p], far_send.at[p], far_recv.at[p], device(-2))

    def relay(p):
        sem = far_send.at[patches + p]
        return remote(near.at[0, p], far.at[p], sem, far_recv.at[p], device(-1))

    def to_hop(look, p):
        slot = look * (patches // 2) + p // 2
        return remote(own.at[look, p], hop.at[slot], hop_send.at[slot], hop_recv.at[slot], device(2))

    def onward_near(look, p):
        slot = look * (patches // 2) + p // 2
        at = look * patches + p
        return remote(hop.at[slot], near.at[look, p], onward_send.at[slot], near_recv.at[at], device(-3))

    def onward_far(p):
        slot = p // 2
        return remote(hop.at[slot], far.at[p], onward_send.at[slot], far_recv.at[p], device(-4))

    def each_route(look, p, act):
        via = jnp.logical_and(crossing, p % 2 == 1)
        via_near = jnp.logical_and(via, jnp.logical_not(odd))
        has_far = jnp.logical_and(odd, look == 0)
        via_far = jnp.logical_and(via, has_far)

        @pl.when(look == sent_look)
        def _():
            act(to_opp(p))

        @pl.when(jnp.logical_or(via_near, via_far))
        def _():
            act(to_hop(look, p))

        @pl.when(jnp.logical_not(via_near))
        def _():
            act(to_near(look, p))

        @pl.when(jnp.logical_and(has_far, jnp.logical_not(via)))
        def _():
            act(to_far(p))

    def send(look, p):
        each_route(look, p, lambda copy: copy.start())

    for look in range(looks):
        energy[look] = jnp.zeros((8, 128), jnp.float32)

    def forward(u, carry):
        look, p = u // patches, u % patches
        load_u = pltpu.make_async_copy(img_ref.at[look, p], img.at[u], img_sem.at[u])
        load_u.wait()
        spec_even, spec_odd = spectrum_of(img.at[u], left_ref, right_ref)
        quarter = BAND // 2
        own[look, p, 0, :, :quarter] = spec_even[:, :quarter]
        own[look, p, 0, :, quarter:] = spec_odd[:, :quarter]
        own[look, p, 1, :, :quarter] = spec_even[:, quarter:]
        own[look, p, 1, :, quarter:] = spec_odd[:, quarter:]
        energy[look] += w_ref[p] * squares_of(spec_even, spec_odd)

        @pl.when(u > 0)
        def _():
            send((u - 1) // patches, (u - 1) % patches)

        return carry

    tables[0].wait()
    tables[1].wait()
    lax.fori_loop(0, looks * patches, forward, 0)
    send(looks - 1, patches - 1)

    tell = []
    for d, look_by in enumerate((0, 1, 2, half)):
        for by in range(nswath):
            if look_by or by:
                tell.append(remote(energy, heard.at[d, by], heard_send.at[d, by], heard_recv.at[d, by],
                                   device(-look_by, by)))
    for copy in tell:
        copy.start()

    rows = WIN // nswath
    mine = pl.ds(pl.multiple_of(lane * rows, rows), rows)

    def outgoing(slot, by):
        at = pl.ds(pl.multiple_of(lax.rem(lane + by, nswath) * rows, rows), rows)
        return remote(outbox.at[slot, at], inbox.at[by - 1, slot], box_send.at[by - 1, slot],
                      box_recv.at[by - 1, slot], device(0, by))

    def returned(by):
        at = pl.ds(pl.multiple_of(lax.rem(lane + by, nswath) * rows, rows), rows)
        return remote(outbox.at[PAIRS, at], backbox.at[by], back_send.at[by], back_recv.at[by],
                      device(half, by))

    def pair(slot, a, b_ref):
        cross_into(w_ref, own.at[a], b_ref, cre, cim)
        keep, turn = halves(first_ref, second_ref, cre, cim)
        value = keep - turn
        surf[slot] = value
        outbox[slot] = value.astype(jnp.bfloat16)
        if slot == PAIRS - 1:
            outbox[PAIRS] = (keep + turn).astype(jnp.bfloat16)
            for by in range(nswath):
                returned(by).start()
        for by in range(1, nswath):
            outgoing(slot, by).start()

    tables[2].wait()
    tables[3].wait()
    pair(0, 0, own.at[1])

    @pl.when(jnp.logical_not(crossing))
    def _():
        for look in range(looks):
            for p in range(1, patches, 2):

                @pl.when(jnp.logical_not(odd))
                def _():
                    to_hop(look, p).wait_recv()
                    onward_near(look, p).start()

                if look == 0:

                    @pl.when(odd)
                    def _():
                        to_hop(look, p).wait_recv()
                        onward_far(p).start()

    for p in range(patches):
        to_near(0, p).wait_recv()

        @pl.when(odd)
        def _():
            relay(p).start()

    pair(1, 0, near.at[0])
    pair(3, 1, near.at[0])

    for copy in tell:
        copy.wait_recv()
    total = []
    for d in range(4):
        for look in range(looks):
            parts = energy[look] if d == 0 else heard[d, 0, look]
            for by in range(1, nswath):
                parts = parts + heard[d, by, look]
            total.append(jnp.sum(parts, axis=(0, 1), keepdims=True))
    scale = BAND * math.sqrt(patches * nswath)

    def factor(look, lag):
        mate = total[look + lag + 1] if lag < 3 else total[3 * looks + look]
        return mask_ref[look, lag].astype(jnp.float32) * scale / jnp.sqrt(total[look] * mate)

    def summed(slot):
        value = surf[slot, mine, :]
        for by in range(1, nswath):
            outgoing(slot, by).wait_recv()
            value = value + inbox[by - 1, slot].astype(jnp.float32)
        return value

    def finish(slot):
        out_ref[slot // 3, slot % 3] = summed(slot) * factor(slot // 3, slot % 3)

    for p in range(patches):
        to_far(p).wait_recv()
    pair(5, 1, far)
    finish(0)
    finish(1)
    finish(3)
    for p in range(patches):
        to_near(1, p).wait_recv()
    pair(2, 0, near.at[1])
    pair(4, 1, near.at[1])
    finish(5)
    for p in range(patches):
        to_opp(p).wait_recv()
    pair(6, kept_look, opp)
    finish(2)
    finish(4)
    kept = summed(PAIRS - 1)
    back = jnp.zeros((rows, WIN), jnp.float32)
    for by in range(nswath):
        returned(by).wait_recv()
        back = back + backbox[by].astype(jnp.float32)
    out_ref[0, 3] = jnp.where(low, kept, back) * factor(0, 3)
    out_ref[1, 3] = jnp.where(low, back, kept) * factor(1, 3)

    for look in range(looks):
        for p in range(patches):
            each_route(look, p, lambda copy: copy.wait_send())
    for p in range(patches):

        @pl.when(odd)
        def _():
            relay(p).wait_send()

    @pl.when(jnp.logical_not(crossing))
    def _():
        for look in range(looks):
            for p in range(1, patches, 2):

                @pl.when(jnp.logical_not(odd))
                def _():
                    onward_near(look, p).wait_send()

                if look == 0:

                    @pl.when(odd)
                    def _():
                        onward_far(p).wait_send()

    for copy in tell:
        copy.wait_send()
    for by in range(nswath):
        returned(by).wait_send()
    for slot in range(PAIRS):
        for by in range(1, nswath):
            outgoing(slot, by).wait_send()


def per_device(images, patch_weight, pair_mask):
    nlook = lax.axis_size("look")
    nswath = lax.axis_size("swath")
    looks, patches = images.shape[:2]
    left, right = forward_tables()
    first, second = inverse_tables()
    rows = WIN // nswath
    vmem = pl.BlockSpec(memory_space=pltpu.VMEM)
    smem = pl.BlockSpec(memory_space=pltpu.SMEM)
    dma = pltpu.SemaphoreType.DMA
    unit = (2, BAND, BAND)
    others = max(nswath - 1, 1)
    return pl.pallas_call(
        functools.partial(kernel, nlook, nswath),
        in_specs=[smem, smem] + [pl.BlockSpec(memory_space=pltpu.HBM)] * 5,
        out_specs=vmem,
        out_shape=jax.ShapeDtypeStruct((looks, 4, rows, WIN), jnp.float32),
        scratch_shapes=[
            pltpu.VMEM(left.shape, jnp.bfloat16),
            pltpu.VMEM(right.shape, jnp.bfloat16),
            pltpu.VMEM(first.shape, jnp.bfloat16),
            pltpu.VMEM(second.shape, jnp.bfloat16),
            pltpu.VMEM((looks * patches, 2, PIX, PIX), jnp.bfloat16),
            pltpu.VMEM((looks * (patches // 2),) + unit, jnp.bfloat16),
            pltpu.VMEM((looks, patches) + unit, jnp.bfloat16),
            pltpu.VMEM((looks, patches) + unit, jnp.bfloat16),
            pltpu.VMEM((patches,) + unit, jnp.bfloat16),
            pltpu.VMEM((patches,) + unit, jnp.bfloat16),
            pltpu.VMEM((looks, 8, 128), jnp.float32),
            pltpu.VMEM((4, nswath, looks, 8, 128), jnp.float32),
            pltpu.VMEM((BAND, BAND), jnp.bfloat16),
            pltpu.VMEM((BAND, BAND), jnp.bfloat16),
            pltpu.VMEM((PAIRS, WIN, WIN), jnp.float32),
            pltpu.VMEM((PAIRS + 1, WIN, WIN), jnp.bfloat16),
            pltpu.VMEM((others, PAIRS, rows, WIN), jnp.bfloat16),
            pltpu.VMEM((nswath, rows, WIN), jnp.bfloat16),
            dma((4,)),
            dma((looks * (patches // 2),)),
            dma((looks * (patches // 2),)),
            dma((looks * (patches // 2),)),
            dma((looks * patches,)),
            dma((looks * patches,)),
            dma((looks * patches,)),
            dma((2 * patches,)),
            dma((patches,)),
            dma((patches,)),
            dma((patches,)),
            dma((4, nswath)),
            dma((4, nswath)),
            dma((others, PAIRS)),
            dma((others, PAIRS)),
            dma((nswath,)),
            dma((nswath,)),
        ],
        compiler_params=pltpu.CompilerParams(
            collective_id=0, has_side_effects=True, vmem_limit_bytes=67043328
        ),
        name="autofocus",
    )(patch_weight, pair_mask, images, left, right, first, second)


def solution(mesh):
    return jax.shard_map(
        per_device,
        mesh=mesh,
        in_specs=(P("look", "swath", None, None, None), P("swath"), P("look", None)),
        out_specs=P("look", None, "swath", None),
        check_vma=False,
    )
```

```python
import functools
import math

import jax
import jax.numpy as jnp
import numpy as np
from jax import lax
from jax.experimental import pallas as pl
from jax.experimental.pallas import tpu as pltpu
from jax.sharding import PartitionSpec as P

PIX = 512
BAND = 256
WIN = 256
HALF = PIX // 2


def phases(rows, cols, row_shift, col_shift):
    phase = (rows[:, None] - row_shift) * (cols[None, :] - col_shift) % PIX
    angle = 2.0 * math.pi / PIX * phase
    return np.cos(angle), np.sin(angle)


def forward_tables():
    left, right = [], []
    for parity in (0, 1):
        re, im = phases(np.arange(parity, BAND, 2), np.arange(HALF), BAND // 2, 0)
        im = -im
        left.append(np.block([[re, -im], [im, re]]))
        right.append(np.block([[re.T, im.T], [-im.T, re.T]]))
    return jnp.asarray(np.stack(left), jnp.bfloat16), jnp.asarray(np.stack(right), jnp.bfloat16)


def inverse_tables():
    order = np.concatenate([np.arange(0, BAND, 2), np.arange(1, BAND, 2)])
    re, im = phases(np.arange(WIN), order, WIN // 2, BAND // 2)
    first = np.concatenate([re, im], axis=0)
    second = np.stack([re.T, im.T])
    return jnp.asarray(first, jnp.bfloat16), jnp.asarray(second, jnp.bfloat16)


def dot(left, right):
    return jnp.dot(left, right, preferred_element_type=jnp.float32)


ROWS = 32
MESH = pl.DeviceIdType.MESH


def spectrum_of(img, left_ref, right_ref):
    re0, re1 = img[0, :HALF, :], img[0, HALF:, :]
    im0, im1 = img[1, :HALF, :], img[1, HALF:, :]
    even = dot(left_ref[0], jnp.concatenate([re0 + re1, im0 + im1], axis=0))
    odd = dot(left_ref[1], jnp.concatenate([re0 - re1, im0 - im1], axis=0))
    quarter = BAND // 2
    parts = []
    for at in (0, quarter):
        parts.append(jnp.concatenate([even[at : at + quarter], odd[at : at + quarter]], axis=0))
    plus = [(part[:, :HALF] + part[:, HALF:]).astype(jnp.bfloat16) for part in parts]
    minus = [(part[:, :HALF] - part[:, HALF:]).astype(jnp.bfloat16) for part in parts]
    spec_even = dot(jnp.concatenate(plus, axis=1), right_ref[0]).astype(jnp.bfloat16)
    spec_odd = dot(jnp.concatenate(minus, axis=1), right_ref[1]).astype(jnp.bfloat16)
    return spec_even, spec_odd


def squares_of(spec_even, spec_odd):
    total = spec_even.astype(jnp.float32) ** 2 + spec_odd.astype(jnp.float32) ** 2
    folded = jnp.sum(total.reshape(BAND // 8, 8, BAND), axis=0)
    return folded[:, : BAND // 2] + folded[:, BAND // 2 :]


def cross_into(w_ref, a_ref, b_ref, cre, cim):
    patches = a_ref.shape[0]

    def step(i, carry):
        rows = pl.ds(pl.multiple_of(i * ROWS, ROWS), ROWS)
        re = jnp.zeros((ROWS, BAND), jnp.float32)
        im = jnp.zeros((ROWS, BAND), jnp.float32)
        for p in range(patches):
            weight = w_ref[p]
            ar = a_ref[p, 0, rows, :].astype(jnp.float32) * weight
            ai = a_ref[p, 1, rows, :].astype(jnp.float32) * weight
            br = b_ref[p, 0, rows, :].astype(jnp.float32)
            bi = b_ref[p, 1, rows, :].astype(jnp.float32)
            re += ar * br + ai * bi
            im += ai * br - ar * bi
        cre[rows, :] = re.astype(jnp.bfloat16)
        cim[rows, :] = im.astype(jnp.bfloat16)
        return carry

    lax.fori_loop(0, BAND // ROWS, step, 0)


def halves(first_ref, second_ref, cre, cim):
    from_re = dot(first_ref[...], cre[...]).astype(jnp.bfloat16)
    from_im = dot(first_ref[...], cim[...]).astype(jnp.bfloat16)
    keep = dot(from_re[:WIN], second_ref[0]) - dot(from_re[WIN:], second_ref[1])
    turn = dot(from_im[:WIN], second_ref[1]) + dot(from_im[WIN:], second_ref[0])
    return keep, turn


PAIRS = 7


def kernel(nlook, nswath, w_ref, mask_ref, img_ref, left_hbm, right_hbm, first_hbm, second_hbm, out_ref, factor_ref,
           left_ref, right_ref, first_ref, second_ref, img, hop, own, near, far, opp, energy, heard, cre, cim, surf, outbox, inbox, backbox,
           table_sem, hop_send, hop_recv, onward_send, img_sem, near_send, near_recv, far_send, far_recv, opp_send, opp_recv,
           heard_send, heard_recv, box_send, box_recv, back_send, back_recv):
    looks, patches = img_ref.shape[:2]
    half = nlook // 2
    me, lane = lax.axis_index("look"), lax.axis_index("swath")
    odd = lax.rem(me, 2) == 1
    crossing = lax.rem(me, 4) < 2
    low = me < half
    sent_look = jnp.where(low, 1, 0)
    kept_look = 1 - sent_look

    def device(look_by, swath_by=0):
        return (lax.rem(me + look_by + nlook, nlook), lax.rem(lane + swath_by, nswath))

    def look_at(u):
        return jnp.where(u // patches == 0, sent_look, kept_look)

    def load(u):
        return pltpu.make_async_copy(img_ref.at[look_at(u), u % patches], img.at[u], img_sem.at[u])

    tables = [
        pltpu.make_async_copy(src, dst, table_sem.at[i])
        for i, (src, dst) in enumerate(
            ((left_hbm, left_ref), (right_hbm, right_ref), (first_hbm, first_ref), (second_hbm, second_ref))
        )
    ]
    load(0).start()
    tables[0].start()
    tables[1].start()
    for u in range(1, looks * patches):
        load(u).start()
    tables[2].start()
    tables[3].start()

    barrier = pltpu.get_barrier_semaphore()
    greeted = 0
    for look_by in (0, 1, -1, 2, -2, half):
        for by in range(nswath):
            if look_by or by:
                greeted += 1
                pl.semaphore_signal(barrier, inc=1, device_id=device(look_by, by), device_id_type=MESH)
    for look_by in (3, -3, 4, -4):
        greeted += 1
        pl.semaphore_signal(barrier, inc=1, device_id=device(look_by), device_id_type=MESH)
    pl.semaphore_wait(barrier, greeted)

    def remote(src, dst, send, recv, to):
        return pltpu.make_async_remote_copy(
            src_ref=src, dst_ref=dst, send_sem=send, recv_sem=recv, device_id=to, device_id_type=MESH
        )

    def to_near(look, p):
        at = look * patches + p
        return remote(own.at[look, p], near.at[look, p], near_send.at[at], near_recv.at[at], device(-1))

    def to_opp(p):
        return remote(own.at[sent_look, p], opp.at[p], opp_send.at[p], opp_recv.at[p], device(half))

    def to_far(p):
        return remote(own.at[0, p], far.at[p], far_send.at[p], far_recv.at[p], device(-2))

    def relay(p):
        sem = far_send.at[patches + p]
        return remote(near.at[0, p], far.at[p], sem, far_recv.at[p], device(-1))

    def to_hop(look, p):
        slot = look * (patches // 2) + p // 2
        return remote(own.at[look, p], hop.at[slot], hop_send.at[slot], hop_recv.at[slot], device(2))

    def onward_near(look, p):
        slot = look * (patches // 2) + p // 2
        at = look * patches + p
        return remote(hop.at[slot], near.at[look, p], onward_send.at[slot], near_recv.at[at], device(-3))

    def onward_far(p):
        slot = p // 2
        return remote(hop.at[slot], far.at[p], onward_send.at[slot], far_recv.at[p], device(-4))

    def each_route(look, p, act):
        via = jnp.logical_and(crossing, p % 2 == 1)
        via_near = jnp.logical_and(via, jnp.logical_not(odd))
        has_far = jnp.logical_and(odd, look == 0)
        via_far = jnp.logical_and(via, has_far)

        @pl.when(jnp.logical_or(via_near, via_far))
        def _():
            act(to_hop(look, p))

        @pl.when(jnp.logical_not(via_near))
        def _():
            act(to_near(look, p))

        @pl.when(jnp.logical_and(has_far, jnp.logical_not(via)))
        def _():
            act(to_far(p))

    def send(u):
        p = u % patches

        @pl.when(u < patches)
        def _():
            to_opp(p).start()

        @pl.when(u >= patches)
        def _():
            for look in range(looks):
                each_route(look, p, lambda copy: copy.start())

    for look in range(looks):
        energy[look] = jnp.zeros((8, 128), jnp.float32)

    def forward(u, carry):
        look, p = look_at(u), u % patches
        load(u).wait()
        spec_even, spec_odd = spectrum_of(img.at[u], left_ref, right_ref)
        quarter = BAND // 2
        own[look, p, 0, :, :quarter] = spec_even[:, :quarter]
        own[look, p, 0, :, quarter:] = spec_odd[:, :quarter]
        own[look, p, 1, :, :quarter] = spec_even[:, quarter:]
        own[look, p, 1, :, quarter:] = spec_odd[:, quarter:]
        energy[look] += w_ref[p] * squares_of(spec_even, spec_odd)

        @pl.when(u > 0)
        def _():
            send(u - 1)

        return carry

    tables[0].wait()
    tables[1].wait()
    lax.fori_loop(0, looks * patches, forward, 0)
    send(looks * patches - 1)

    tell = []
    for d, look_by in enumerate((0, 1, 2, half)):
        for by in range(nswath):
            if look_by or by:
                tell.append(remote(energy, heard.at[d, by], heard_send.at[d, by], heard_recv.at[d, by],
                                   device(-look_by, by)))
    for copy in tell:
        copy.start()

    rows = WIN // nswath
    mine = pl.ds(pl.multiple_of(lane * rows, rows), rows)

    def outgoing(slot, by):
        at = pl.ds(pl.multiple_of(lax.rem(lane + by, nswath) * rows, rows), rows)
        return remote(outbox.at[slot, at], inbox.at[by - 1, slot], box_send.at[by - 1, slot],
                      box_recv.at[by - 1, slot], device(0, by))

    def returned(by):
        at = pl.ds(pl.multiple_of(lax.rem(lane + by, nswath) * rows, rows), rows)
        return remote(outbox.at[PAIRS, at], backbox.at[by], back_send.at[by], back_recv.at[by],
                      device(half, by))

    def pair(slot, a, b_ref):
        cross_into(w_ref, own.at[a], b_ref, cre, cim)
        keep, turn = halves(first_ref, second_ref, cre, cim)
        value = keep - turn
        surf[slot] = value
        outbox[slot] = value.astype(jnp.bfloat16)
        if slot == PAIRS - 1:
            outbox[PAIRS] = (keep + turn).astype(jnp.bfloat16)
            for by in range(nswath):
                returned(by).start()
        for by in range(1, nswath):
            outgoing(slot, by).start()

    tables[2].wait()
    tables[3].wait()
    pair(0, 0, own.at[1])

    @pl.when(jnp.logical_not(crossing))
    def _():
        for look in range(looks):
            for p in range(1, patches, 2):

                @pl.when(jnp.logical_not(odd))
                def _():
                    to_hop(look, p).wait_recv()
                    onward_near(look, p).start()

                if look == 0:

                    @pl.when(odd)
                    def _():
                        to_hop(look, p).wait_recv()
                        onward_far(p).start()

    for p in range(patches):
        to_opp(p).wait_recv()
    pair(6, kept_look, opp)
    for p in range(patches):
        to_near(0, p).wait_recv()

        @pl.when(odd)
        def _():
            relay(p).start()

    pair(1, 0, near.at[0])
    pair(3, 1, near.at[0])

    for copy in tell:
        copy.wait_recv()
    total = []
    for d in range(4):
        for look in range(looks):
            parts = energy[look] if d == 0 else heard[d, 0, look]
            for by in range(1, nswath):
                parts = parts + heard[d, by, look]
            total.append(jnp.sum(parts, axis=(0, 1), keepdims=True))
    scale = BAND * math.sqrt(patches * nswath)

    def factor(look, lag):
        mate = total[look + lag + 1] if lag < 3 else total[3 * looks + look]
        return mask_ref[look, lag].astype(jnp.float32) * scale / jnp.sqrt(total[look] * mate)

    def summed(slot):
        value = surf[slot, mine, :]
        for by in range(1, nswath):
            outgoing(slot, by).wait_recv()
            value = value + inbox[by - 1, slot].astype(jnp.float32)
        return value

    def finish(slot):
        out_ref[slot // 3, slot % 3] = summed(slot)

    for look in range(looks):
        for lag in range(4):
            at = look * 4 + lag
            factor_ref[at : at + 1, :] = jnp.broadcast_to(factor(look, lag), (1, 128))
    finish(0)
    for p in range(patches):
        to_near(1, p).wait_recv()
    pair(2, 0, near.at[1])
    pair(4, 1, near.at[1])
    finish(1)
    finish(3)
    for p in range(patches):
        to_far(p).wait_recv()
    pair(5, 1, far)
    kept = summed(PAIRS - 1)
    back = jnp.zeros((rows, WIN), jnp.float32)
    for by in range(nswath):
        returned(by).wait_recv()
        back = back + backbox[by].astype(jnp.float32)
    out_ref[0, 3] = jnp.where(low, kept, back)
    out_ref[1, 3] = jnp.where(low, back, kept)
    finish(2)
    finish(4)
    finish(5)

    for look in range(looks):
        for p in range(patches):
            each_route(look, p, lambda copy: copy.wait_send())
    for p in range(patches):
        to_opp(p).wait_send()

        @pl.when(odd)
        def _():
            relay(p).wait_send()

    @pl.when(jnp.logical_not(crossing))
    def _():
        for look in range(looks):
            for p in range(1, patches, 2):

                @pl.when(jnp.logical_not(odd))
                def _():
                    onward_near(look, p).wait_send()

                if look == 0:

                    @pl.when(odd)
                    def _():
                        onward_far(p).wait_send()

    for copy in tell:
        copy.wait_send()
    for by in range(nswath):
        returned(by).wait_send()
    for slot in range(PAIRS):
        for by in range(1, nswath):
            outgoing(slot, by).wait_send()


def per_device(images, patch_weight, pair_mask):
    nlook = lax.axis_size("look")
    nswath = lax.axis_size("swath")
    looks, patches = images.shape[:2]
    left, right = forward_tables()
    first, second = inverse_tables()
    rows = WIN // nswath
    vmem = pl.BlockSpec(memory_space=pltpu.VMEM)
    smem = pl.BlockSpec(memory_space=pltpu.SMEM)
    dma = pltpu.SemaphoreType.DMA
    unit = (2, BAND, BAND)
    others = max(nswath - 1, 1)
    surfaces, factors = pl.pallas_call(
        functools.partial(kernel, nlook, nswath),
        in_specs=[smem, smem] + [pl.BlockSpec(memory_space=pltpu.HBM)] * 5,
        out_specs=[vmem, vmem],
        out_shape=[
            jax.ShapeDtypeStruct((looks, 4, rows, WIN), jnp.float32),
            jax.ShapeDtypeStruct((looks * 4, 128), jnp.float32),
        ],
        scratch_shapes=[
            pltpu.VMEM(left.shape, jnp.bfloat16),
            pltpu.VMEM(right.shape, jnp.bfloat16),
            pltpu.VMEM(first.shape, jnp.bfloat16),
            pltpu.VMEM(second.shape, jnp.bfloat16),
            pltpu.VMEM((looks * patches, 2, PIX, PIX), jnp.bfloat16),
            pltpu.VMEM((looks * (patches // 2),) + unit, jnp.bfloat16),
            pltpu.VMEM((looks, patches) + unit, jnp.bfloat16),
            pltpu.VMEM((looks, patches) + unit, jnp.bfloat16),
            pltpu.VMEM((patches,) + unit, jnp.bfloat16),
            pltpu.VMEM((patches,) + unit, jnp.bfloat16),
            pltpu.VMEM((looks, 8, 128), jnp.float32),
            pltpu.VMEM((4, nswath, looks, 8, 128), jnp.float32),
            pltpu.VMEM((BAND, BAND), jnp.bfloat16),
            pltpu.VMEM((BAND, BAND), jnp.bfloat16),
            pltpu.VMEM((PAIRS, WIN, WIN), jnp.float32),
            pltpu.VMEM((PAIRS + 1, WIN, WIN), jnp.bfloat16),
            pltpu.VMEM((others, PAIRS, rows, WIN), jnp.bfloat16),
            pltpu.VMEM((nswath, rows, WIN), jnp.bfloat16),
            dma((4,)),
            dma((looks * (patches // 2),)),
            dma((looks * (patches // 2),)),
            dma((looks * (patches // 2),)),
            dma((looks * patches,)),
            dma((looks * patches,)),
            dma((looks * patches,)),
            dma((2 * patches,)),
            dma((patches,)),
            dma((patches,)),
            dma((patches,)),
            dma((4, nswath)),
            dma((4, nswath)),
            dma((others, PAIRS)),
            dma((others, PAIRS)),
            dma((nswath,)),
            dma((nswath,)),
        ],
        compiler_params=pltpu.CompilerParams(
            collective_id=0, has_side_effects=True, vmem_limit_bytes=67043328
        ),
        name="autofocus",
    )(patch_weight, pair_mask, images, left, right, first, second)
    return surfaces * factors[:, 0].reshape(looks, 4)[:, :, None, None]


def solution(mesh):
    return jax.shard_map(
        per_device,
        mesh=mesh,
        in_specs=(P("look", "swath", None, None, None), P("swath"), P("look", None)),
        out_specs=P("look", None, "swath", None),
        check_vma=False,
    )
```

```python
import functools
import math

import jax
import jax.numpy as jnp
import numpy as np
from jax import lax
from jax.experimental import pallas as pl
from jax.experimental.pallas import tpu as pltpu
from jax.sharding import PartitionSpec as P

PIX = 512
BAND = 256
WIN = 256
HALF = PIX // 2


def phases(rows, cols, row_shift, col_shift):
    phase = (rows[:, None] - row_shift) * (cols[None, :] - col_shift) % PIX
    angle = 2.0 * math.pi / PIX * phase
    return np.cos(angle), np.sin(angle)


def forward_tables():
    left, right = [], []
    for parity in (0, 1):
        re, im = phases(np.arange(parity, BAND, 2), np.arange(HALF), BAND // 2, 0)
        im = -im
        left.append(np.block([[re, -im], [im, re]]))
        right.append(np.block([[re.T, im.T], [-im.T, re.T]]))
    return jnp.asarray(np.stack(left), jnp.bfloat16), jnp.asarray(np.stack(right), jnp.bfloat16)


def inverse_tables():
    order = np.concatenate([np.arange(0, BAND, 2), np.arange(1, BAND, 2)])
    re, im = phases(np.arange(WIN), order, WIN // 2, BAND // 2)
    first = np.concatenate([re, im], axis=0)
    second = np.stack([re.T, im.T])
    return jnp.asarray(first, jnp.bfloat16), jnp.asarray(second, jnp.bfloat16)


def dot(left, right):
    return jnp.dot(left, right, preferred_element_type=jnp.float32)


ROWS = 32
MESH = pl.DeviceIdType.MESH


def spectrum_of(img, left_ref, right_ref):
    re0, re1 = img[0, :HALF, :], img[0, HALF:, :]
    im0, im1 = img[1, :HALF, :], img[1, HALF:, :]
    even = dot(left_ref[0], jnp.concatenate([re0 + re1, im0 + im1], axis=0))
    odd = dot(left_ref[1], jnp.concatenate([re0 - re1, im0 - im1], axis=0))
    quarter = BAND // 2
    parts = []
    for at in (0, quarter):
        parts.append(jnp.concatenate([even[at : at + quarter], odd[at : at + quarter]], axis=0))
    plus = [(part[:, :HALF] + part[:, HALF:]).astype(jnp.bfloat16) for part in parts]
    minus = [(part[:, :HALF] - part[:, HALF:]).astype(jnp.bfloat16) for part in parts]
    spec_even = dot(jnp.concatenate(plus, axis=1), right_ref[0]).astype(jnp.bfloat16)
    spec_odd = dot(jnp.concatenate(minus, axis=1), right_ref[1]).astype(jnp.bfloat16)
    return spec_even, spec_odd


def squares_of(spec_even, spec_odd):
    total = spec_even.astype(jnp.float32) ** 2 + spec_odd.astype(jnp.float32) ** 2
    folded = jnp.sum(total.reshape(BAND // 8, 8, BAND), axis=0)
    return folded[:, : BAND // 2] + folded[:, BAND // 2 :]


def cross_into(w_ref, a_ref, b_ref, cre, cim):
    patches = a_ref.shape[0]

    def step(i, carry):
        rows = pl.ds(pl.multiple_of(i * ROWS, ROWS), ROWS)
        re = jnp.zeros((ROWS, BAND), jnp.float32)
        im = jnp.zeros((ROWS, BAND), jnp.float32)
        for p in range(patches):
            weight = w_ref[p]
            ar = a_ref[p, 0, rows, :].astype(jnp.float32) * weight
            ai = a_ref[p, 1, rows, :].astype(jnp.float32) * weight
            br = b_ref[p, 0, rows, :].astype(jnp.float32)
            bi = b_ref[p, 1, rows, :].astype(jnp.float32)
            re += ar * br + ai * bi
            im += ai * br - ar * bi
        cre[rows, :] = re.astype(jnp.bfloat16)
        cim[rows, :] = im.astype(jnp.bfloat16)
        return carry

    lax.fori_loop(0, BAND // ROWS, step, 0)


def halves(first_ref, second_ref, cre, cim):
    from_re = dot(first_ref[...], cre[...]).astype(jnp.bfloat16)
    from_im = dot(first_ref[...], cim[...]).astype(jnp.bfloat16)
    keep = dot(from_re[:WIN], second_ref[0]) - dot(from_re[WIN:], second_ref[1])
    turn = dot(from_im[:WIN], second_ref[1]) + dot(from_im[WIN:], second_ref[0])
    return keep, turn


PAIRS = 7
LAST = PAIRS - 1


def kernel(nlook, nswath, w_ref, mask_ref, img_ref, left_hbm, right_hbm, first_hbm, second_hbm, out_ref, factor_ref,
           left_ref, right_ref, first_ref, second_ref, img, hop, own, near, far, opp, energy, heard, cre, cim, surf, outbox, inbox, turned, backbox,
           table_sem, hop_send, hop_recv, onward_send, forward_send, img_sem, near_send, near_recv, far_send, far_recv, opp_send, opp_recv,
           heard_send, heard_recv, box_send, box_recv, back_send, back_recv):
    looks, patches = img_ref.shape[:2]
    half = nlook // 2
    me, lane = lax.axis_index("look"), lax.axis_index("swath")
    odd = lax.rem(me, 2) == 1
    crossing = lax.rem(me, 4) < 2
    low = me < half
    sent_look = jnp.where(low, 1, 0)
    kept_look = 1 - sent_look

    def device(look_by, swath_by=0):
        return (lax.rem(me + look_by + nlook, nlook), lax.rem(lane + swath_by, nswath))

    def look_at(u):
        return jnp.where(u // patches == 0, sent_look, kept_look)

    def load(u):
        return pltpu.make_async_copy(img_ref.at[look_at(u), u % patches], img.at[u], img_sem.at[u])

    tables = [
        pltpu.make_async_copy(src, dst, table_sem.at[i])
        for i, (src, dst) in enumerate(
            ((left_hbm, left_ref), (right_hbm, right_ref), (first_hbm, first_ref), (second_hbm, second_ref))
        )
    ]
    load(0).start()
    tables[0].start()
    tables[1].start()
    for u in range(1, looks * patches):
        load(u).start()
    tables[2].start()
    tables[3].start()

    barrier = pltpu.get_barrier_semaphore()
    greeted = 0
    for look_by in (0, 1, -1, 2, -2, half):
        for by in range(nswath):
            if look_by or by:
                greeted += 1
                pl.semaphore_signal(barrier, inc=1, device_id=device(look_by, by), device_id_type=MESH)
    for look_by in (3, -3, 4, -4, half - 1, 1 - half, half - 2, 2 - half):
        greeted += 1
        pl.semaphore_signal(barrier, inc=1, device_id=device(look_by), device_id_type=MESH)
    pl.semaphore_wait(barrier, greeted)

    def remote(src, dst, send, recv, to):
        return pltpu.make_async_remote_copy(
            src_ref=src, dst_ref=dst, send_sem=send, recv_sem=recv, device_id=to, device_id_type=MESH
        )

    def to_near(look, p):
        at = look * patches + p
        return remote(own.at[look, p], near.at[look, p], near_send.at[at], near_recv.at[at], device(-1))

    def to_opp(p):
        return remote(own.at[sent_look, p], opp.at[p], opp_send.at[p], opp_recv.at[p], device(half))

    def to_far(p):
        return remote(own.at[0, p], far.at[p], far_send.at[p], far_recv.at[p], device(-2))

    def relay(p):
        sem = far_send.at[patches + p]
        return remote(near.at[0, p], far.at[p], sem, far_recv.at[p], device(-1))

    def to_hop(look, p):
        slot = look * (patches // 2) + p // 2
        return remote(own.at[look, p], hop.at[slot], hop_send.at[slot], hop_recv.at[slot], device(2))

    def onward_near(look, p):
        slot = look * (patches // 2) + p // 2
        at = look * patches + p
        return remote(hop.at[slot], near.at[look, p], onward_send.at[slot], near_recv.at[at], device(-3))

    def onward_far(p):
        slot = p // 2
        return remote(hop.at[slot], far.at[p], onward_send.at[slot], far_recv.at[p], device(-4))

    def forwarded_near(source, look):
        low_one = jnp.logical_and(source == 0, look == 1)
        return jnp.logical_or(low_one, jnp.logical_and(source == half, look == 0))

    def each_forward(p, act):
        at = forward_send.at[p]

        @pl.when(me == 0)
        def _():
            act(remote(opp.at[p], near.at[0, p], at, near_recv.at[p], device(half - 1)))

        @pl.when(me == 1)
        def _():
            act(remote(opp.at[p], far.at[p], at, far_recv.at[p], device(half - 2)))

        @pl.when(me == half)
        def _():
            act(remote(opp.at[p], near.at[1, p], at, near_recv.at[patches + p], device(half - 1)))

    def each_onward(act):
        for look in range(looks):
            for p in range(1, patches, 2):

                @pl.when(jnp.logical_not(jnp.logical_or(odd, forwarded_near(me - 2, look))))
                def _():
                    act(look, p, onward_near(look, p))

                if look == 0:

                    @pl.when(jnp.logical_and(odd, me != half + 3))
                    def _():
                        act(look, p, onward_far(p))

    def each_route(look, p, act):
        via = jnp.logical_and(crossing, p % 2 == 1)
        has_near = jnp.logical_not(forwarded_near(me, look))
        via_near = jnp.logical_and(jnp.logical_and(via, has_near), jnp.logical_not(odd))
        has_far = jnp.logical_and(jnp.logical_and(odd, look == 0), me != half + 1)
        via_far = jnp.logical_and(via, has_far)

        @pl.when(jnp.logical_or(via_near, via_far))
        def _():
            act(to_hop(look, p))

        @pl.when(jnp.logical_and(has_near, jnp.logical_not(via_near)))
        def _():
            act(to_near(look, p))

        @pl.when(jnp.logical_and(has_far, jnp.logical_not(via)))
        def _():
            act(to_far(p))

    def send(u):
        p = u % patches

        @pl.when(u < patches)
        def _():
            to_opp(p).start()

        @pl.when(u >= patches)
        def _():
            early = p < patches // 2
            look = jnp.where(early, sent_look, kept_look)
            for step in range(2):
                patch = 2 * lax.rem(p, patches // 2) + step
                each_route(look, patch, lambda copy: copy.start())

    for look in range(looks):
        energy[look] = jnp.zeros((8, 128), jnp.float32)

    def forward(u, carry):
        look, p = look_at(u), u % patches
        load(u).wait()
        spec_even, spec_odd = spectrum_of(img.at[u], left_ref, right_ref)
        quarter = BAND // 2
        own[look, p, 0, :, :quarter] = spec_even[:, :quarter]
        own[look, p, 0, :, quarter:] = spec_odd[:, :quarter]
        own[look, p, 1, :, :quarter] = spec_even[:, quarter:]
        own[look, p, 1, :, quarter:] = spec_odd[:, quarter:]
        energy[look] += w_ref[p] * squares_of(spec_even, spec_odd)

        @pl.when(u > 0)
        def _():
            send(u - 1)

        return carry

    tables[0].wait()
    tables[1].wait()
    lax.fori_loop(0, looks * patches, forward, 0)
    send(looks * patches - 1)

    tell = []
    for d, look_by in enumerate((0, 1, 2, half)):
        for by in range(nswath):
            if look_by or by:
                tell.append(remote(energy, heard.at[d, by], heard_send.at[d, by], heard_recv.at[d, by],
                                   device(-look_by, by)))
    for copy in tell:
        copy.start()

    rows = WIN // nswath
    mine = pl.ds(pl.multiple_of(lane * rows, rows), rows)

    def outgoing(slot, by):
        at = pl.ds(pl.multiple_of(lax.rem(lane + by, nswath) * rows, rows), rows)
        return remote(outbox.at[slot, at], inbox.at[by - 1, slot], box_send.at[by - 1, slot],
                      box_recv.at[by - 1, slot], device(0, by))

    def returned():
        return remote(turned, backbox, back_send.at[0], back_recv.at[0], device(half))

    def pair(slot, a, b_ref):
        cross_into(w_ref, own.at[a], b_ref, cre, cim)
        keep, turn = halves(first_ref, second_ref, cre, cim)
        value = keep - turn
        surf[slot] = value
        outbox[slot] = value.astype(jnp.bfloat16)
        both = slot is LAST
        if both:
            value = keep + turn
            surf[PAIRS] = value
            outbox[PAIRS] = value.astype(jnp.bfloat16)
        for by in range(1, nswath):
            if both:
                outgoing(PAIRS, by).start()
            outgoing(slot, by).start()

    tables[2].wait()
    tables[3].wait()
    pair(0, 0, own.at[1])

    @pl.when(jnp.logical_not(crossing))
    def _():
        def onward(look, p, copy):
            to_hop(look, p).wait_recv()
            copy.start()

        each_onward(onward)

    for p in range(patches):
        to_opp(p).wait_recv()
        each_forward(p, lambda copy: copy.start())
    pair(LAST, kept_look, opp)

    for copy in tell:
        copy.wait_recv()
    total = []
    for d in range(4):
        for look in range(looks):
            parts = energy[look] if d == 0 else heard[d, 0, look]
            for by in range(1, nswath):
                parts = parts + heard[d, by, look]
            total.append(jnp.sum(parts, axis=(0, 1), keepdims=True))
    scale = BAND * math.sqrt(patches * nswath)

    def factor(look, lag):
        mate = total[look + lag + 1] if lag < 3 else total[3 * looks + look]
        return mask_ref[look, lag].astype(jnp.float32) * scale / jnp.sqrt(total[look] * mate)

    def summed(slot):
        value = surf[slot, mine, :]
        for by in range(1, nswath):
            outgoing(slot, by).wait_recv()
            value = value + inbox[by - 1, slot].astype(jnp.float32)
        return value

    def finish(slot):
        out_ref[slot // 3, slot % 3] = summed(slot)

    turned[...] = summed(PAIRS).astype(jnp.bfloat16)
    for look in range(looks):
        for lag in range(4):
            at = look * 4 + lag
            factor_ref[at : at + 1, :] = jnp.broadcast_to(factor(look, lag), (1, 128))
    finish(0)
    returned().start()
    ahead = lax.rem(me + 1, nlook)
    first_look = jnp.where(ahead < half, 1, 0)
    for look in (first_look, 1 - first_look):
        for p in range(patches):
            to_near(look, p).wait_recv()

            @pl.when(jnp.logical_and(odd, look == 0))
            def _():
                relay(p).start()

        pair(1 + look, 0, near.at[look])
        pair(3 + look, 1, near.at[look])
    for p in range(patches):
        to_far(p).wait_recv()
    pair(5, 1, far)
    finish(1)
    finish(3)
    kept = summed(PAIRS - 1)
    returned().wait_recv()
    back = backbox[...].astype(jnp.float32)
    out_ref[0, 3] = jnp.where(low, kept, back)
    out_ref[1, 3] = jnp.where(low, back, kept)
    finish(2)
    finish(4)
    finish(5)

    for look in range(looks):
        for p in range(patches):
            each_route(look, p, lambda copy: copy.wait_send())
    for p in range(patches):
        to_opp(p).wait_send()

        @pl.when(odd)
        def _():
            relay(p).wait_send()

        each_forward(p, lambda copy: copy.wait_send())

    @pl.when(jnp.logical_not(crossing))
    def _():
        each_onward(lambda look, p, copy: copy.wait_send())

    for copy in tell:
        copy.wait_send()
    returned().wait_send()
    for slot in range(PAIRS + 1):
        for by in range(1, nswath):
            outgoing(slot, by).wait_send()


def per_device(images, patch_weight, pair_mask):
    nlook = lax.axis_size("look")
    nswath = lax.axis_size("swath")
    looks, patches = images.shape[:2]
    left, right = forward_tables()
    first, second = inverse_tables()
    rows = WIN // nswath
    vmem = pl.BlockSpec(memory_space=pltpu.VMEM)
    smem = pl.BlockSpec(memory_space=pltpu.SMEM)
    dma = pltpu.SemaphoreType.DMA
    unit = (2, BAND, BAND)
    others = max(nswath - 1, 1)
    surfaces, factors = pl.pallas_call(
        functools.partial(kernel, nlook, nswath),
        in_specs=[smem, smem] + [pl.BlockSpec(memory_space=pltpu.HBM)] * 5,
        out_specs=[vmem, vmem],
        out_shape=[
            jax.ShapeDtypeStruct((looks, 4, rows, WIN), jnp.float32),
            jax.ShapeDtypeStruct((looks * 4, 128), jnp.float32),
        ],
        scratch_shapes=[
            pltpu.VMEM(left.shape, jnp.bfloat16),
            pltpu.VMEM(right.shape, jnp.bfloat16),
            pltpu.VMEM(first.shape, jnp.bfloat16),
            pltpu.VMEM(second.shape, jnp.bfloat16),
            pltpu.VMEM((looks * patches, 2, PIX, PIX), jnp.bfloat16),
            pltpu.VMEM((looks * (patches // 2),) + unit, jnp.bfloat16),
            pltpu.VMEM((looks, patches) + unit, jnp.bfloat16),
            pltpu.VMEM((looks, patches) + unit, jnp.bfloat16),
            pltpu.VMEM((patches,) + unit, jnp.bfloat16),
            pltpu.VMEM((patches,) + unit, jnp.bfloat16),
            pltpu.VMEM((looks, 8, 128), jnp.float32),
            pltpu.VMEM((4, nswath, looks, 8, 128), jnp.float32),
            pltpu.VMEM((BAND, BAND), jnp.bfloat16),
            pltpu.VMEM((BAND, BAND), jnp.bfloat16),
            pltpu.VMEM((PAIRS + 1, WIN, WIN), jnp.float32),
            pltpu.VMEM((PAIRS + 1, WIN, WIN), jnp.bfloat16),
            pltpu.VMEM((others, PAIRS + 1, rows, WIN), jnp.bfloat16),
            pltpu.VMEM((rows, WIN), jnp.bfloat16),
            pltpu.VMEM((rows, WIN), jnp.bfloat16),
            dma((4,)),
            dma((looks * (patches // 2),)),
            dma((looks * (patches // 2),)),
            dma((looks * (patches // 2),)),
            dma((patches,)),
            dma((looks * patches,)),
            dma((looks * patches,)),
            dma((looks * patches,)),
            dma((2 * patches,)),
            dma((patches,)),
            dma((patches,)),
            dma((patches,)),
            dma((4, nswath)),
            dma((4, nswath)),
            dma((others, PAIRS + 1)),
            dma((others, PAIRS + 1)),
            dma((1,)),
            dma((1,)),
        ],
        compiler_params=pltpu.CompilerParams(
            collective_id=0, has_side_effects=True, vmem_limit_bytes=67043328
        ),
        name="autofocus",
    )(patch_weight, pair_mask, images, left, right, first, second)
    return surfaces * factors[:, 0].reshape(looks, 4)[:, :, None, None]


def solution(mesh):
    return jax.shard_map(
        per_device,
        mesh=mesh,
        in_specs=(P("look", "swath", None, None, None), P("swath"), P("look", None)),
        out_specs=P("look", None, "swath", None),
        check_vma=False,
    )
```

```python
import functools
import math

import jax
import jax.numpy as jnp
import numpy as np
from jax import lax
from jax.experimental import pallas as pl
from jax.experimental.pallas import tpu as pltpu
from jax.sharding import PartitionSpec as P

PIX = 512
BAND = 256
WIN = 256
HALF = PIX // 2


def phases(rows, cols, row_shift, col_shift):
    phase = (rows[:, None] - row_shift) * (cols[None, :] - col_shift) % PIX
    angle = 2.0 * math.pi / PIX * phase
    return np.cos(angle), np.sin(angle)


def forward_tables():
    left, right = [], []
    for parity in (0, 1):
        re, im = phases(np.arange(parity, BAND, 2), np.arange(HALF), BAND // 2, 0)
        im = -im
        left.append(np.block([[re, -im], [im, re]]))
        right.append(np.block([[re.T, im.T], [-im.T, re.T]]))
    return jnp.asarray(np.stack(left), jnp.bfloat16), jnp.asarray(np.stack(right), jnp.bfloat16)


def inverse_tables():
    order = np.concatenate([np.arange(0, BAND, 2), np.arange(1, BAND, 2)])
    re, im = phases(np.arange(WIN), order, WIN // 2, BAND // 2)
    first = np.concatenate([re, im], axis=0)
    second = np.stack([re.T, im.T])
    return jnp.asarray(first, jnp.bfloat16), jnp.asarray(second, jnp.bfloat16)


def dot(left, right):
    return jnp.dot(left, right, preferred_element_type=jnp.float32)


ROWS = 32
MESH = pl.DeviceIdType.MESH


def spectrum_of(img, left_ref, right_ref):
    re0, re1 = img[0, :HALF, :], img[0, HALF:, :]
    im0, im1 = img[1, :HALF, :], img[1, HALF:, :]
    even = dot(left_ref[0], jnp.concatenate([re0 + re1, im0 + im1], axis=0))
    odd = dot(left_ref[1], jnp.concatenate([re0 - re1, im0 - im1], axis=0))
    quarter = BAND // 2
    parts = []
    for at in (0, quarter):
        parts.append(jnp.concatenate([even[at : at + quarter], odd[at : at + quarter]], axis=0))
    plus = [(part[:, :HALF] + part[:, HALF:]).astype(jnp.bfloat16) for part in parts]
    minus = [(part[:, :HALF] - part[:, HALF:]).astype(jnp.bfloat16) for part in parts]
    spec_even = dot(jnp.concatenate(plus, axis=1), right_ref[0]).astype(jnp.bfloat16)
    spec_odd = dot(jnp.concatenate(minus, axis=1), right_ref[1]).astype(jnp.bfloat16)
    return spec_even, spec_odd


def squares_of(spec_even, spec_odd):
    total = spec_even.astype(jnp.float32) ** 2 + spec_odd.astype(jnp.float32) ** 2
    folded = jnp.sum(total.reshape(BAND // 8, 8, BAND), axis=0)
    return folded[:, : BAND // 2] + folded[:, BAND // 2 :]


def cross_into(w_ref, a_ref, b_ref, cre, cim):
    patches = a_ref.shape[0]

    def step(i, carry):
        rows = pl.ds(pl.multiple_of(i * ROWS, ROWS), ROWS)
        re = jnp.zeros((ROWS, BAND), jnp.float32)
        im = jnp.zeros((ROWS, BAND), jnp.float32)
        for p in range(patches):
            weight = w_ref[p]
            ar = a_ref[p, 0, rows, :].astype(jnp.float32) * weight
            ai = a_ref[p, 1, rows, :].astype(jnp.float32) * weight
            br = b_ref[p, 0, rows, :].astype(jnp.float32)
            bi = b_ref[p, 1, rows, :].astype(jnp.float32)
            re += ar * br + ai * bi
            im += ai * br - ar * bi
        cre[rows, :] = re.astype(jnp.bfloat16)
        cim[rows, :] = im.astype(jnp.bfloat16)
        return carry

    lax.fori_loop(0, BAND // ROWS, step, 0)


def halves(first_ref, second_ref, cre, cim):
    from_re = dot(first_ref[...], cre[...]).astype(jnp.bfloat16)
    from_im = dot(first_ref[...], cim[...]).astype(jnp.bfloat16)
    keep = dot(from_re[:WIN], second_ref[0]) - dot(from_re[WIN:], second_ref[1])
    turn = dot(from_im[:WIN], second_ref[1]) + dot(from_im[WIN:], second_ref[0])
    return keep, turn


PAIRS = 7
LAST = PAIRS - 1


def kernel(nlook, nswath, w_ref, mask_ref, img_ref, left_hbm, right_hbm, first_hbm, second_hbm, out_ref, factor_ref,
           left_ref, right_ref, first_ref, second_ref, img, hop, own, near, far, opp, energy, heard, cre, cim, surf, outbox, inbox, turned, backbox,
           table_sem, hop_send, hop_recv, onward_send, forward_send, img_sem, near_send, near_recv, far_send, far_recv, opp_send, opp_recv,
           heard_send, heard_recv, box_send, box_recv, back_send, back_recv):
    looks, patches = img_ref.shape[:2]
    half = nlook // 2
    me, lane = lax.axis_index("look"), lax.axis_index("swath")
    odd = lax.rem(me, 2) == 1
    crossing = lax.rem(me, 4) < 2
    low = me < half
    sent_look = jnp.where(low, 1, 0)
    kept_look = 1 - sent_look

    def device(look_by, swath_by=0):
        return (lax.rem(me + look_by + nlook, nlook), lax.rem(lane + swath_by, nswath))

    def look_at(u):
        return jnp.where(u // patches == 0, sent_look, kept_look)

    def load(u):
        return pltpu.make_async_copy(img_ref.at[look_at(u), u % patches], img.at[u], img_sem.at[u])

    tables = [
        pltpu.make_async_copy(src, dst, table_sem.at[i])
        for i, (src, dst) in enumerate(
            ((left_hbm, left_ref), (right_hbm, right_ref), (first_hbm, first_ref), (second_hbm, second_ref))
        )
    ]
    load(0).start()
    tables[0].start()
    tables[1].start()
    for u in range(1, looks * patches):
        load(u).start()
    tables[2].start()
    tables[3].start()

    barrier = pltpu.get_barrier_semaphore()
    greeted = 0
    for look_by in (0, 1, -1, 2, -2, half):
        for by in range(nswath):
            if look_by or by:
                greeted += 1
                pl.semaphore_signal(barrier, inc=1, device_id=device(look_by, by), device_id_type=MESH)
    for look_by in (3, -3, 4, -4, half - 1, 1 - half, half - 2, 2 - half):
        greeted += 1
        pl.semaphore_signal(barrier, inc=1, device_id=device(look_by), device_id_type=MESH)
    pl.semaphore_wait(barrier, greeted)

    def remote(src, dst, send, recv, to):
        return pltpu.make_async_remote_copy(
            src_ref=src, dst_ref=dst, send_sem=send, recv_sem=recv, device_id=to, device_id_type=MESH
        )

    def to_near(look, p):
        at = look * patches + p
        return remote(own.at[look, p], near.at[look, p], near_send.at[at], near_recv.at[at], device(-1))

    def to_opp(p):
        return remote(own.at[sent_look, p], opp.at[p], opp_send.at[p], opp_recv.at[p], device(half))

    def to_far(p):
        return remote(own.at[0, p], far.at[p], far_send.at[p], far_recv.at[p], device(-2))

    def relay(p):
        sem = far_send.at[patches + p]
        return remote(near.at[0, p], far.at[p], sem, far_recv.at[p], device(-1))

    def to_hop(look, p):
        slot = look * (patches // 2) + p // 2
        return remote(own.at[look, p], hop.at[slot], hop_send.at[slot], hop_recv.at[slot], device(2))

    def onward_near(look, p):
        slot = look * (patches // 2) + p // 2
        at = look * patches + p
        return remote(hop.at[slot], near.at[look, p], onward_send.at[slot], near_recv.at[at], device(-3))

    def onward_far(p):
        slot = p // 2
        return remote(hop.at[slot], far.at[p], onward_send.at[slot], far_recv.at[p], device(-4))

    def forwarded_near(source, look):
        low_one = jnp.logical_and(source == 0, look == 1)
        return jnp.logical_or(low_one, jnp.logical_and(source == half, look == 0))

    def each_forward(p, act):
        at = forward_send.at[p]

        @pl.when(me == 0)
        def _():
            act(remote(opp.at[p], near.at[0, p], at, near_recv.at[p], device(half - 1)))

        @pl.when(me == 1)
        def _():
            act(remote(opp.at[p], far.at[p], at, far_recv.at[p], device(half - 2)))

        @pl.when(me == half)
        def _():
            act(remote(opp.at[p], near.at[1, p], at, near_recv.at[patches + p], device(half - 1)))

    def each_onward(act):
        for look in range(looks):
            for p in range(1, patches, 2):

                @pl.when(jnp.logical_not(jnp.logical_or(odd, forwarded_near(me - 2, look))))
                def _():
                    act(look, p, onward_near(look, p))

                if look == 0:

                    @pl.when(jnp.logical_and(odd, me != half + 3))
                    def _():
                        act(look, p, onward_far(p))

    def each_route(look, p, act):
        via = jnp.logical_and(crossing, p % 2 == 1)
        has_near = jnp.logical_not(forwarded_near(me, look))
        via_near = jnp.logical_and(jnp.logical_and(via, has_near), jnp.logical_not(odd))
        has_far = jnp.logical_and(jnp.logical_and(odd, look == 0), me != half + 1)
        via_far = jnp.logical_and(via, has_far)

        @pl.when(jnp.logical_or(via_near, via_far))
        def _():
            act(to_hop(look, p))

        @pl.when(jnp.logical_and(has_near, jnp.logical_not(via_near)))
        def _():
            act(to_near(look, p))

        @pl.when(jnp.logical_and(has_far, jnp.logical_not(via)))
        def _():
            act(to_far(p))

    def send(u):
        p = u % patches

        @pl.when(u < patches)
        def _():
            to_opp(p).start()

        @pl.when(u >= patches)
        def _():
            early = p < patches // 2
            look = jnp.where(early, sent_look, kept_look)
            for step in range(2):
                patch = 2 * lax.rem(p, patches // 2) + step
                each_route(look, patch, lambda copy: copy.start())

    for look in range(looks):
        energy[look] = jnp.zeros((8, 128), jnp.float32)

    def forward(u, carry):
        look, p = look_at(u), u % patches
        load(u).wait()
        spec_even, spec_odd = spectrum_of(img.at[u], left_ref, right_ref)
        quarter = BAND // 2
        own[look, p, 0, :, :quarter] = spec_even[:, :quarter]
        own[look, p, 0, :, quarter:] = spec_odd[:, :quarter]
        own[look, p, 1, :, :quarter] = spec_even[:, quarter:]
        own[look, p, 1, :, quarter:] = spec_odd[:, quarter:]
        energy[look] += w_ref[p] * squares_of(spec_even, spec_odd)

        @pl.when(u > 0)
        def _():
            send(u - 1)

        return carry

    tables[0].wait()
    tables[1].wait()
    lax.fori_loop(0, looks * patches, forward, 0)
    send(looks * patches - 1)

    tell = []
    for d, look_by in enumerate((0, 1, 2, half)):
        for by in range(nswath):
            if look_by or by:
                tell.append(remote(energy, heard.at[d, by], heard_send.at[d, by], heard_recv.at[d, by],
                                   device(-look_by, by)))
    for copy in tell:
        copy.start()

    rows = WIN // nswath
    mine = pl.ds(pl.multiple_of(lane * rows, rows), rows)

    def outgoing(slot, by):
        at = pl.ds(pl.multiple_of(lax.rem(lane + by, nswath) * rows, rows), rows)
        return remote(outbox.at[slot, at], inbox.at[by - 1, slot], box_send.at[by - 1, slot],
                      box_recv.at[by - 1, slot], device(0, by))

    def returned():
        return remote(turned, backbox, back_send.at[0], back_recv.at[0], device(half))

    def pair(slot, a, b_ref):
        cross_into(w_ref, own.at[a], b_ref, cre, cim)
        keep, turn = halves(first_ref, second_ref, cre, cim)
        value = keep - turn
        surf[slot] = value
        outbox[slot] = value.astype(jnp.bfloat16)
        both = slot is LAST
        if both:
            value = keep + turn
            surf[PAIRS] = value
            outbox[PAIRS] = value.astype(jnp.bfloat16)
        for by in range(1, nswath):
            if both:
                outgoing(PAIRS, by).start()
            outgoing(slot, by).start()

    tables[2].wait()
    tables[3].wait()
    pair(0, 0, own.at[1])

    @pl.when(jnp.logical_not(crossing))
    def _():
        def onward(look, p, copy):
            to_hop(look, p).wait_recv()
            copy.start()

        each_onward(onward)

    late = jnp.logical_and(odd, jnp.logical_not(crossing))

    def ring_pairs():
        ahead = lax.rem(me + 1, nlook)
        first_look = jnp.where(ahead < half, 1, 0)
        for look in (first_look, 1 - first_look):
            for p in range(patches):
                to_near(look, p).wait_recv()

                @pl.when(jnp.logical_and(odd, look == 0))
                def _():
                    relay(p).start()

            pair(1 + look, 0, near.at[look])
            pair(3 + look, 1, near.at[look])
    @pl.when(jnp.logical_not(late))
    def _():
        ring_pairs()

    for p in range(patches):
        to_opp(p).wait_recv()
        each_forward(p, lambda copy: copy.start())
    pair(LAST, kept_look, opp)

    for copy in tell:
        copy.wait_recv()
    total = []
    for d in range(4):
        for look in range(looks):
            parts = energy[look] if d == 0 else heard[d, 0, look]
            for by in range(1, nswath):
                parts = parts + heard[d, by, look]
            total.append(jnp.sum(parts, axis=(0, 1), keepdims=True))
    scale = BAND * math.sqrt(patches * nswath)

    def factor(look, lag):
        mate = total[look + lag + 1] if lag < 3 else total[3 * looks + look]
        return mask_ref[look, lag].astype(jnp.float32) * scale / jnp.sqrt(total[look] * mate)

    def summed(slot):
        value = surf[slot, mine, :]
        for by in range(1, nswath):
            outgoing(slot, by).wait_recv()
            value = value + inbox[by - 1, slot].astype(jnp.float32)
        return value

    def finish(slot):
        out_ref[slot // 3, slot % 3] = summed(slot)

    turned[...] = summed(PAIRS).astype(jnp.bfloat16)
    for look in range(looks):
        for lag in range(4):
            factor_ref[look, lag] = jnp.broadcast_to(factor(look, lag), (1, WIN))
    finish(0)
    returned().start()

    @pl.when(late)
    def _():
        ring_pairs()

    for p in range(patches):
        to_far(p).wait_recv()
    pair(5, 1, far)
    finish(1)
    finish(3)
    kept = summed(PAIRS - 1)
    returned().wait_recv()
    back = backbox[...].astype(jnp.float32)
    out_ref[0, 3] = jnp.where(low, kept, back)
    out_ref[1, 3] = jnp.where(low, back, kept)
    finish(2)
    finish(4)
    finish(5)

    for look in range(looks):
        for p in range(patches):
            each_route(look, p, lambda copy: copy.wait_send())
    for p in range(patches):
        to_opp(p).wait_send()

        @pl.when(odd)
        def _():
            relay(p).wait_send()

        each_forward(p, lambda copy: copy.wait_send())

    @pl.when(jnp.logical_not(crossing))
    def _():
        each_onward(lambda look, p, copy: copy.wait_send())

    for copy in tell:
        copy.wait_send()
    returned().wait_send()
    for slot in range(PAIRS + 1):
        for by in range(1, nswath):
            outgoing(slot, by).wait_send()


def per_device(images, patch_weight, pair_mask):
    nlook = lax.axis_size("look")
    nswath = lax.axis_size("swath")
    looks, patches = images.shape[:2]
    left, right = forward_tables()
    first, second = inverse_tables()
    rows = WIN // nswath
    vmem = pl.BlockSpec(memory_space=pltpu.VMEM)
    smem = pl.BlockSpec(memory_space=pltpu.SMEM)
    dma = pltpu.SemaphoreType.DMA
    unit = (2, BAND, BAND)
    others = max(nswath - 1, 1)
    surfaces, factors = pl.pallas_call(
        functools.partial(kernel, nlook, nswath),
        in_specs=[smem, smem] + [pl.BlockSpec(memory_space=pltpu.HBM)] * 5,
        out_specs=[vmem, vmem],
        out_shape=[
            jax.ShapeDtypeStruct((looks, 4, rows, WIN), jnp.float32),
            jax.ShapeDtypeStruct((looks, 4, 1, WIN), jnp.float32),
        ],
        scratch_shapes=[
            pltpu.VMEM(left.shape, jnp.bfloat16),
            pltpu.VMEM(right.shape, jnp.bfloat16),
            pltpu.VMEM(first.shape, jnp.bfloat16),
            pltpu.VMEM(second.shape, jnp.bfloat16),
            pltpu.VMEM((looks * patches, 2, PIX, PIX), jnp.bfloat16),
            pltpu.VMEM((looks * (patches // 2),) + unit, jnp.bfloat16),
            pltpu.VMEM((looks, patches) + unit, jnp.bfloat16),
            pltpu.VMEM((looks, patches) + unit, jnp.bfloat16),
            pltpu.VMEM((patches,) + unit, jnp.bfloat16),
            pltpu.VMEM((patches,) + unit, jnp.bfloat16),
            pltpu.VMEM((looks, 8, 128), jnp.float32),
            pltpu.VMEM((4, nswath, looks, 8, 128), jnp.float32),
            pltpu.VMEM((BAND, BAND), jnp.bfloat16),
            pltpu.VMEM((BAND, BAND), jnp.bfloat16),
            pltpu.VMEM((PAIRS + 1, WIN, WIN), jnp.float32),
            pltpu.VMEM((PAIRS + 1, WIN, WIN), jnp.bfloat16),
            pltpu.VMEM((others, PAIRS + 1, rows, WIN), jnp.bfloat16),
            pltpu.VMEM((rows, WIN), jnp.bfloat16),
            pltpu.VMEM((rows, WIN), jnp.bfloat16),
            dma((4,)),
            dma((looks * (patches // 2),)),
            dma((looks * (patches // 2),)),
            dma((looks * (patches // 2),)),
            dma((patches,)),
            dma((looks * patches,)),
            dma((looks * patches,)),
            dma((looks * patches,)),
            dma((2 * patches,)),
            dma((patches,)),
            dma((patches,)),
            dma((patches,)),
            dma((4, nswath)),
            dma((4, nswath)),
            dma((others, PAIRS + 1)),
            dma((others, PAIRS + 1)),
            dma((1,)),
            dma((1,)),
        ],
        compiler_params=pltpu.CompilerParams(
            collective_id=0, has_side_effects=True, vmem_limit_bytes=67043328
        ),
        name="autofocus",
    )(patch_weight, pair_mask, images, left, right, first, second)
    return surfaces * factors


def solution(mesh):
    return jax.shard_map(
        per_device,
        mesh=mesh,
        in_specs=(P("look", "swath", None, None, None), P("swath"), P("look", None)),
        out_specs=P("look", None, "swath", None),
        check_vma=False,
    )
```

```python
import functools
import math

import jax
import jax.numpy as jnp
import numpy as np
from jax import lax
from jax.experimental import pallas as pl
from jax.experimental.pallas import tpu as pltpu
from jax.sharding import PartitionSpec as P

PIX = 512
BAND = 256
WIN = 256
HALF = PIX // 2


def phases(rows, cols, row_shift, col_shift):
    phase = (rows[:, None] - row_shift) * (cols[None, :] - col_shift) % PIX
    angle = 2.0 * math.pi / PIX * phase
    return np.cos(angle), np.sin(angle)


def forward_tables():
    left, right = [], []
    for parity in (0, 1):
        re, im = phases(np.arange(parity, BAND, 2), np.arange(HALF), BAND // 2, 0)
        im = -im
        left.append(np.block([[re, -im], [im, re]]))
        right.append(np.block([[re.T, im.T], [-im.T, re.T]]))
    return jnp.asarray(np.stack(left), jnp.bfloat16), jnp.asarray(np.stack(right), jnp.bfloat16)


def inverse_tables():
    order = np.concatenate([np.arange(0, BAND, 2), np.arange(1, BAND, 2)])
    re, im = phases(np.arange(WIN), order, WIN // 2, BAND // 2)
    first = np.concatenate([re, im], axis=0)
    second = np.stack([re.T, im.T])
    return jnp.asarray(first, jnp.bfloat16), jnp.asarray(second, jnp.bfloat16)


def dot(left, right):
    return jnp.dot(left, right, preferred_element_type=jnp.float32)


ROWS = 32
MESH = pl.DeviceIdType.MESH


def spectrum_of(img, left_ref, right_ref):
    re0, re1 = img[0, :HALF, :], img[0, HALF:, :]
    im0, im1 = img[1, :HALF, :], img[1, HALF:, :]
    even = dot(left_ref[0], jnp.concatenate([re0 + re1, im0 + im1], axis=0))
    odd = dot(left_ref[1], jnp.concatenate([re0 - re1, im0 - im1], axis=0))
    quarter = BAND // 2
    parts = []
    for at in (0, quarter):
        parts.append(jnp.concatenate([even[at : at + quarter], odd[at : at + quarter]], axis=0))
    plus = [(part[:, :HALF] + part[:, HALF:]).astype(jnp.bfloat16) for part in parts]
    minus = [(part[:, :HALF] - part[:, HALF:]).astype(jnp.bfloat16) for part in parts]
    spec_even = dot(jnp.concatenate(plus, axis=1), right_ref[0]).astype(jnp.bfloat16)
    spec_odd = dot(jnp.concatenate(minus, axis=1), right_ref[1]).astype(jnp.bfloat16)
    return spec_even, spec_odd


def squares_of(spec_even, spec_odd):
    total = spec_even.astype(jnp.float32) ** 2 + spec_odd.astype(jnp.float32) ** 2
    folded = jnp.sum(total.reshape(BAND // 8, 8, BAND), axis=0)
    return folded[:, : BAND // 2] + folded[:, BAND // 2 :]


def cross_into(w_ref, a_ref, b_ref, cre, cim):
    patches = a_ref.shape[0]

    def step(i, carry):
        rows = pl.ds(pl.multiple_of(i * ROWS, ROWS), ROWS)
        re = jnp.zeros((ROWS, BAND), jnp.float32)
        im = jnp.zeros((ROWS, BAND), jnp.float32)
        for p in range(patches):
            weight = w_ref[p]
            ar = a_ref[p, 0, rows, :].astype(jnp.float32) * weight
            ai = a_ref[p, 1, rows, :].astype(jnp.float32) * weight
            br = b_ref[p, 0, rows, :].astype(jnp.float32)
            bi = b_ref[p, 1, rows, :].astype(jnp.float32)
            re += ar * br + ai * bi
            im += ai * br - ar * bi
        cre[rows, :] = re.astype(jnp.bfloat16)
        cim[rows, :] = im.astype(jnp.bfloat16)
        return carry

    lax.fori_loop(0, BAND // ROWS, step, 0)


def halves(first_ref, second_ref, cre, cim):
    from_re = dot(first_ref[...], cre[...]).astype(jnp.bfloat16)
    from_im = dot(first_ref[...], cim[...]).astype(jnp.bfloat16)
    keep = dot(from_re[:WIN], second_ref[0]) - dot(from_re[WIN:], second_ref[1])
    turn = dot(from_im[:WIN], second_ref[1]) + dot(from_im[WIN:], second_ref[0])
    return keep, turn


PAIRS = 7
LAST = PAIRS - 1


def kernel(nlook, nswath, w_ref, mask_ref, img_ref, left_hbm, right_hbm, first_hbm, second_hbm, out_ref, factor_ref,
           left_ref, right_ref, first_ref, second_ref, img, hop, own, near, far, opp, energy, heard, cre, cim, surf, outbox, inbox, turned, backbox,
           table_sem, hop_send, hop_recv, onward_send, forward_send, img_sem, near_send, near_recv, far_send, far_recv, opp_send, opp_recv,
           heard_send, heard_recv, box_send, box_recv, back_send, back_recv):
    looks, patches = img_ref.shape[:2]
    half = nlook // 2
    me, lane = lax.axis_index("look"), lax.axis_index("swath")
    odd = lax.rem(me, 2) == 1
    crossing = lax.rem(me, 4) < 2
    low = me < half
    sent_look = jnp.where(low, 1, 0)
    kept_look = 1 - sent_look

    def device(look_by, swath_by=0):
        return (lax.rem(me + look_by + nlook, nlook), lax.rem(lane + swath_by, nswath))

    def look_at(u):
        return jnp.where(u // patches == 0, sent_look, kept_look)

    def load(u):
        return pltpu.make_async_copy(img_ref.at[look_at(u), u % patches], img.at[u], img_sem.at[u])

    tables = [
        pltpu.make_async_copy(src, dst, table_sem.at[i])
        for i, (src, dst) in enumerate(
            ((left_hbm, left_ref), (right_hbm, right_ref), (first_hbm, first_ref), (second_hbm, second_ref))
        )
    ]
    load(0).start()
    tables[0].start()
    tables[1].start()
    for u in range(1, looks * patches):
        load(u).start()
    tables[2].start()
    tables[3].start()

    barrier = pltpu.get_barrier_semaphore()
    greeted = 0
    for look_by in (0, 1, -1, 2, -2, half):
        for by in range(nswath):
            if look_by or by:
                greeted += 1
                pl.semaphore_signal(barrier, inc=1, device_id=device(look_by, by), device_id_type=MESH)
    for look_by in (3, -3, 4, -4, half - 1, 1 - half, half - 2, 2 - half):
        greeted += 1
        pl.semaphore_signal(barrier, inc=1, device_id=device(look_by), device_id_type=MESH)
    pl.semaphore_wait(barrier, greeted)

    def remote(src, dst, send, recv, to):
        return pltpu.make_async_remote_copy(
            src_ref=src, dst_ref=dst, send_sem=send, recv_sem=recv, device_id=to, device_id_type=MESH
        )

    def to_near(look, p):
        at = look * patches + p
        return remote(own.at[look, p], near.at[look, p], near_send.at[at], near_recv.at[at], device(-1))

    def to_opp(p):
        return remote(own.at[sent_look, p], opp.at[p], opp_send.at[p], opp_recv.at[p], device(half))

    def to_far(p):
        return remote(own.at[0, p], far.at[p], far_send.at[p], far_recv.at[p], device(-2))

    def relay(p):
        sem = far_send.at[patches + p]
        return remote(near.at[0, p], far.at[p], sem, far_recv.at[p], device(-1))

    def to_hop(look, p):
        slot = look * (patches // 2) + p // 2
        return remote(own.at[look, p], hop.at[slot], hop_send.at[slot], hop_recv.at[slot], device(2))

    def onward_near(look, p):
        slot = look * (patches // 2) + p // 2
        at = look * patches + p
        return remote(hop.at[slot], near.at[look, p], onward_send.at[slot], near_recv.at[at], device(-3))

    def onward_far(p):
        slot = p // 2
        return remote(hop.at[slot], far.at[p], onward_send.at[slot], far_recv.at[p], device(-4))

    def forwarded_near(source, look):
        low_one = jnp.logical_and(source == 0, look == 1)
        return jnp.logical_or(low_one, jnp.logical_and(source == half, look == 0))

    def each_forward(p, act):
        at = forward_send.at[p]

        @pl.when(me == 0)
        def _():
            act(remote(opp.at[p], near.at[0, p], at, near_recv.at[p], device(half - 1)))

        @pl.when(me == 1)
        def _():
            act(remote(opp.at[p], far.at[p], at, far_recv.at[p], device(half - 2)))

        @pl.when(me == half)
        def _():
            act(remote(opp.at[p], near.at[1, p], at, near_recv.at[patches + p], device(half - 1)))

    def each_onward(act):
        for look in range(looks):
            for p in range(1, patches, 2):

                @pl.when(jnp.logical_not(jnp.logical_or(odd, forwarded_near(me - 2, look))))
                def _():
                    act(look, p, onward_near(look, p))

                if look == 0:

                    @pl.when(jnp.logical_and(odd, me != half + 3))
                    def _():
                        act(look, p, onward_far(p))

    def each_route(look, p, act):
        via = jnp.logical_and(crossing, p % 2 == 1)
        has_near = jnp.logical_not(forwarded_near(me, look))
        via_near = jnp.logical_and(jnp.logical_and(via, has_near), jnp.logical_not(odd))
        has_far = jnp.logical_and(jnp.logical_and(odd, look == 0), me != half + 1)
        via_far = jnp.logical_and(via, has_far)

        @pl.when(jnp.logical_or(via_near, via_far))
        def _():
            act(to_hop(look, p))

        @pl.when(jnp.logical_and(has_near, jnp.logical_not(via_near)))
        def _():
            act(to_near(look, p))

        @pl.when(jnp.logical_and(has_far, jnp.logical_not(via)))
        def _():
            act(to_far(p))

    def send(u):
        p = u % patches

        @pl.when(u < patches)
        def _():
            to_opp(p).start()

        @pl.when(u >= patches)
        def _():
            early = p < patches // 2
            look = jnp.where(early, sent_look, kept_look)
            for step in range(2):
                patch = 2 * lax.rem(p, patches // 2) + step
                each_route(look, patch, lambda copy: copy.start())

    for look in range(looks):
        energy[look] = jnp.zeros((8, 128), jnp.float32)

    def forward(u, carry):
        @pl.when(u > 0)
        def _():
            send(u - 1)

        look, p = look_at(u), u % patches
        load(u).wait()
        spec_even, spec_odd = spectrum_of(img.at[u], left_ref, right_ref)
        quarter = BAND // 2
        own[look, p, 0, :, :quarter] = spec_even[:, :quarter]
        own[look, p, 0, :, quarter:] = spec_odd[:, :quarter]
        own[look, p, 1, :, :quarter] = spec_even[:, quarter:]
        own[look, p, 1, :, quarter:] = spec_odd[:, quarter:]
        energy[look] += w_ref[p] * squares_of(spec_even, spec_odd)

        return carry

    tables[0].wait()
    tables[1].wait()
    lax.fori_loop(0, looks * patches, forward, 0)
    send(looks * patches - 1)

    tell = []
    for d, look_by in enumerate((0, 1, 2, half)):
        for by in range(nswath):
            if look_by or by:
                tell.append(remote(energy, heard.at[d, by], heard_send.at[d, by], heard_recv.at[d, by],
                                   device(-look_by, by)))
    for copy in tell:
        copy.start()

    rows = WIN // nswath
    mine = pl.ds(pl.multiple_of(lane * rows, rows), rows)

    def outgoing(slot, by):
        at = pl.ds(pl.multiple_of(lax.rem(lane + by, nswath) * rows, rows), rows)
        return remote(outbox.at[slot, at], inbox.at[by - 1, slot], box_send.at[by - 1, slot],
                      box_recv.at[by - 1, slot], device(0, by))

    def returned():
        return remote(turned, backbox, back_send.at[0], back_recv.at[0], device(half))

    def pair(slot, a, b_ref):
        cross_into(w_ref, own.at[a], b_ref, cre, cim)
        keep, turn = halves(first_ref, second_ref, cre, cim)
        value = keep - turn
        surf[slot] = value
        outbox[slot] = value.astype(jnp.bfloat16)
        both = slot is LAST
        if both:
            value = keep + turn
            surf[PAIRS] = value
            outbox[PAIRS] = value.astype(jnp.bfloat16)
        for by in range(1, nswath):
            if both:
                outgoing(PAIRS, by).start()
            outgoing(slot, by).start()

    tables[2].wait()
    tables[3].wait()
    pair(0, 0, own.at[1])

    @pl.when(jnp.logical_not(crossing))
    def _():
        def onward(look, p, copy):
            to_hop(look, p).wait_recv()
            copy.start()

        each_onward(onward)

    late = jnp.logical_and(odd, jnp.logical_not(crossing))

    def ring_pairs():
        ahead = lax.rem(me + 1, nlook)
        first_look = jnp.where(jnp.logical_and(ahead < half, ahead != 0), 1, 0)
        for look in (first_look, 1 - first_look):
            for p in range(patches):
                to_near(look, p).wait_recv()

                @pl.when(jnp.logical_and(odd, look == 0))
                def _():
                    relay(p).start()

            pair(1 + look, 0, near.at[look])
            pair(3 + look, 1, near.at[look])
    @pl.when(jnp.logical_not(late))
    def _():
        ring_pairs()

    for p in range(patches):
        to_opp(p).wait_recv()
        each_forward(p, lambda copy: copy.start())
    pair(LAST, kept_look, opp)

    for copy in tell:
        copy.wait_recv()
    total = []
    for d in range(4):
        for look in range(looks):
            parts = energy[look] if d == 0 else heard[d, 0, look]
            for by in range(1, nswath):
                parts = parts + heard[d, by, look]
            total.append(jnp.sum(parts, axis=(0, 1), keepdims=True))
    scale = BAND * math.sqrt(patches * nswath)

    def factor(look, lag):
        mate = total[look + lag + 1] if lag < 3 else total[3 * looks + look]
        return mask_ref[look, lag].astype(jnp.float32) * scale / jnp.sqrt(total[look] * mate)

    def summed(slot):
        value = surf[slot, mine, :]
        for by in range(1, nswath):
            outgoing(slot, by).wait_recv()
            value = value + inbox[by - 1, slot].astype(jnp.float32)
        return value

    def finish(slot):
        out_ref[slot // 3, slot % 3] = summed(slot)

    turned[...] = summed(PAIRS).astype(jnp.bfloat16)
    for look in range(looks):
        for lag in range(4):
            factor_ref[look, lag : lag + 1, :] = jnp.broadcast_to(factor(look, lag), (1, WIN))
    finish(0)
    returned().start()

    @pl.when(late)
    def _():
        ring_pairs()

    for p in range(patches):
        to_far(p).wait_recv()
    pair(5, 1, far)
    finish(1)
    finish(3)
    kept = summed(PAIRS - 1)
    returned().wait_recv()
    back = backbox[...].astype(jnp.float32)
    out_ref[0, 3] = jnp.where(low, kept, back)
    out_ref[1, 3] = jnp.where(low, back, kept)
    finish(2)
    finish(4)
    finish(5)

    for look in range(looks):
        for p in range(patches):
            each_route(look, p, lambda copy: copy.wait_send())
    for p in range(patches):
        to_opp(p).wait_send()

        @pl.when(odd)
        def _():
            relay(p).wait_send()

        each_forward(p, lambda copy: copy.wait_send())

    @pl.when(jnp.logical_not(crossing))
    def _():
        each_onward(lambda look, p, copy: copy.wait_send())

    for copy in tell:
        copy.wait_send()
    returned().wait_send()
    for slot in range(PAIRS + 1):
        for by in range(1, nswath):
            outgoing(slot, by).wait_send()


def per_device(images, patch_weight, pair_mask):
    nlook = lax.axis_size("look")
    nswath = lax.axis_size("swath")
    looks, patches = images.shape[:2]
    left, right = forward_tables()
    first, second = inverse_tables()
    rows = WIN // nswath
    vmem = pl.BlockSpec(memory_space=pltpu.VMEM)
    smem = pl.BlockSpec(memory_space=pltpu.SMEM)
    dma = pltpu.SemaphoreType.DMA
    unit = (2, BAND, BAND)
    others = max(nswath - 1, 1)
    surfaces, factors = pl.pallas_call(
        functools.partial(kernel, nlook, nswath),
        in_specs=[smem, smem] + [pl.BlockSpec(memory_space=pltpu.HBM)] * 5,
        out_specs=[vmem, vmem],
        out_shape=[
            jax.ShapeDtypeStruct((looks, 4, rows, WIN), jnp.float32),
            jax.ShapeDtypeStruct((looks, 4, WIN), jnp.float32),
        ],
        scratch_shapes=[
            pltpu.VMEM(left.shape, jnp.bfloat16),
            pltpu.VMEM(right.shape, jnp.bfloat16),
            pltpu.VMEM(first.shape, jnp.bfloat16),
            pltpu.VMEM(second.shape, jnp.bfloat16),
            pltpu.VMEM((looks * patches, 2, PIX, PIX), jnp.bfloat16),
            pltpu.VMEM((looks * (patches // 2),) + unit, jnp.bfloat16),
            pltpu.VMEM((looks, patches) + unit, jnp.bfloat16),
            pltpu.VMEM((looks, patches) + unit, jnp.bfloat16),
            pltpu.VMEM((patches,) + unit, jnp.bfloat16),
            pltpu.VMEM((patches,) + unit, jnp.bfloat16),
            pltpu.VMEM((looks, 8, 128), jnp.float32),
            pltpu.VMEM((4, nswath, looks, 8, 128), jnp.float32),
            pltpu.VMEM((BAND, BAND), jnp.bfloat16),
            pltpu.VMEM((BAND, BAND), jnp.bfloat16),
            pltpu.VMEM((PAIRS + 1, WIN, WIN), jnp.float32),
            pltpu.VMEM((PAIRS + 1, WIN, WIN), jnp.bfloat16),
            pltpu.VMEM((others, PAIRS + 1, rows, WIN), jnp.bfloat16),
            pltpu.VMEM((rows, WIN), jnp.bfloat16),
            pltpu.VMEM((rows, WIN), jnp.bfloat16),
            dma((4,)),
            dma((looks * (patches // 2),)),
            dma((looks * (patches // 2),)),
            dma((looks * (patches // 2),)),
            dma((patches,)),
            dma((looks * patches,)),
            dma((looks * patches,)),
            dma((looks * patches,)),
            dma((2 * patches,)),
            dma((patches,)),
            dma((patches,)),
            dma((patches,)),
            dma((4, nswath)),
            dma((4, nswath)),
            dma((others, PAIRS + 1)),
            dma((others, PAIRS + 1)),
            dma((1,)),
            dma((1,)),
        ],
        compiler_params=pltpu.CompilerParams(
            collective_id=0, has_side_effects=True, vmem_limit_bytes=67043328
        ),
        name="autofocus",
    )(patch_weight, pair_mask, images, left, right, first, second)
    return surfaces * factors[:, :, None, :]


def solution(mesh):
    return jax.shard_map(
        per_device,
        mesh=mesh,
        in_specs=(P("look", "swath", None, None, None), P("swath"), P("look", None)),
        out_specs=P("look", None, "swath", None),
        check_vma=False,
    )
```

```python
import functools
import math

import jax
import jax.numpy as jnp
import numpy as np
from jax import lax
from jax.experimental import pallas as pl
from jax.experimental.pallas import tpu as pltpu
from jax.sharding import PartitionSpec as P

PIX = 512
BAND = 256
WIN = 256
HALF = PIX // 2


def phases(rows, cols, row_shift, col_shift):
    phase = (rows[:, None] - row_shift) * (cols[None, :] - col_shift) % PIX
    angle = 2.0 * math.pi / PIX * phase
    return np.cos(angle), np.sin(angle)


def forward_tables():
    left, right = [], []
    for parity in (0, 1):
        re, im = phases(np.arange(parity, BAND, 2), np.arange(HALF), BAND // 2, 0)
        im = -im
        left.append(np.block([[re, -im], [im, re]]))
        right.append(np.block([[re.T, im.T], [-im.T, re.T]]))
    return jnp.asarray(np.stack(left), jnp.bfloat16), jnp.asarray(np.stack(right), jnp.bfloat16)


def inverse_tables():
    order = np.concatenate([np.arange(0, BAND, 2), np.arange(1, BAND, 2)])
    re, im = phases(np.arange(WIN), order, WIN // 2, BAND // 2)
    first = np.concatenate([re, im], axis=0)
    second = np.stack([re.T, im.T])
    return jnp.asarray(first, jnp.bfloat16), jnp.asarray(second, jnp.bfloat16)


def dot(left, right):
    return jnp.dot(left, right, preferred_element_type=jnp.float32)


ROWS = 32
MESH = pl.DeviceIdType.MESH


def spectrum_of(img, left_ref, right_ref):
    re0, re1 = img[0, :HALF, :], img[0, HALF:, :]
    im0, im1 = img[1, :HALF, :], img[1, HALF:, :]
    even = dot(left_ref[0], jnp.concatenate([re0 + re1, im0 + im1], axis=0))
    odd = dot(left_ref[1], jnp.concatenate([re0 - re1, im0 - im1], axis=0))
    quarter = BAND // 2
    parts = []
    for at in (0, quarter):
        parts.append(jnp.concatenate([even[at : at + quarter], odd[at : at + quarter]], axis=0))
    plus = [(part[:, :HALF] + part[:, HALF:]).astype(jnp.bfloat16) for part in parts]
    minus = [(part[:, :HALF] - part[:, HALF:]).astype(jnp.bfloat16) for part in parts]
    spec_even = dot(jnp.concatenate(plus, axis=1), right_ref[0]).astype(jnp.bfloat16)
    spec_odd = dot(jnp.concatenate(minus, axis=1), right_ref[1]).astype(jnp.bfloat16)
    return spec_even, spec_odd


def squares_of(spec_even, spec_odd):
    total = spec_even.astype(jnp.float32) ** 2 + spec_odd.astype(jnp.float32) ** 2
    folded = jnp.sum(total.reshape(BAND // 8, 8, BAND), axis=0)
    return folded[:, : BAND // 2] + folded[:, BAND // 2 :]


def cross_into(w_ref, a_ref, b_ref, cre, cim):
    patches = a_ref.shape[0]

    def step(i, carry):
        rows = pl.ds(pl.multiple_of(i * ROWS, ROWS), ROWS)
        re = jnp.zeros((ROWS, BAND), jnp.float32)
        im = jnp.zeros((ROWS, BAND), jnp.float32)
        for p in range(patches):
            weight = w_ref[p]
            ar = a_ref[p, 0, rows, :].astype(jnp.float32) * weight
            ai = a_ref[p, 1, rows, :].astype(jnp.float32) * weight
            br = b_ref[p, 0, rows, :].astype(jnp.float32)
            bi = b_ref[p, 1, rows, :].astype(jnp.float32)
            re += ar * br + ai * bi
            im += ai * br - ar * bi
        cre[rows, :] = re.astype(jnp.bfloat16)
        cim[rows, :] = im.astype(jnp.bfloat16)
        return carry

    lax.fori_loop(0, BAND // ROWS, step, 0)


def halves(first_ref, second_ref, cre, cim):
    from_re = dot(first_ref[...], cre[...]).astype(jnp.bfloat16)
    from_im = dot(first_ref[...], cim[...]).astype(jnp.bfloat16)
    keep = dot(from_re[:WIN], second_ref[0]) - dot(from_re[WIN:], second_ref[1])
    turn = dot(from_im[:WIN], second_ref[1]) + dot(from_im[WIN:], second_ref[0])
    return keep, turn


PAIRS = 7
LAST = PAIRS - 1


def kernel(nlook, nswath, w_ref, mask_ref, img_ref, left_hbm, right_hbm, first_hbm, second_hbm, out_ref, factor_ref,
           left_ref, right_ref, first_ref, second_ref, img, hop, own, near, far, opp, energy, heard, cre, cim, surf, outbox, inbox, turned, backbox,
           table_sem, hop_send, hop_recv, onward_send, forward_send, img_sem, near_send, near_recv, far_send, far_recv, opp_send, opp_recv,
           heard_send, heard_recv, box_send, box_recv, back_send, back_recv):
    looks, patches = img_ref.shape[:2]
    half = nlook // 2
    me, lane = lax.axis_index("look"), lax.axis_index("swath")
    odd = lax.rem(me, 2) == 1
    crossing = lax.rem(me, 4) < 2
    low = me < half
    sent_look = jnp.where(low, 1, 0)
    kept_look = 1 - sent_look

    def device(look_by, swath_by=0):
        return (lax.rem(me + look_by + nlook, nlook), lax.rem(lane + swath_by, nswath))

    def look_at(u):
        return jnp.where(u // patches == 0, sent_look, kept_look)

    def load(u):
        return pltpu.make_async_copy(img_ref.at[look_at(u), u % patches], img.at[u], img_sem.at[u])

    tables = [
        pltpu.make_async_copy(src, dst, table_sem.at[i])
        for i, (src, dst) in enumerate(
            ((left_hbm, left_ref), (right_hbm, right_ref), (first_hbm, first_ref), (second_hbm, second_ref))
        )
    ]
    load(0).start()
    tables[0].start()
    tables[1].start()
    for u in range(1, looks * patches):
        load(u).start()
    tables[2].start()
    tables[3].start()

    barrier = pltpu.get_barrier_semaphore()
    greeted = 0
    for look_by in (0, 1, -1, 2, -2, half):
        for by in range(nswath):
            if look_by or by:
                greeted += 1
                pl.semaphore_signal(barrier, inc=1, device_id=device(look_by, by), device_id_type=MESH)
    for look_by in (3, -3, 4, -4, half - 1, 1 - half, half - 2, 2 - half):
        greeted += 1
        pl.semaphore_signal(barrier, inc=1, device_id=device(look_by), device_id_type=MESH)
    pl.semaphore_wait(barrier, greeted)

    def remote(src, dst, send, recv, to):
        return pltpu.make_async_remote_copy(
            src_ref=src, dst_ref=dst, send_sem=send, recv_sem=recv, device_id=to, device_id_type=MESH
        )

    def to_near(look, p):
        at = look * patches + p
        return remote(own.at[look, p], near.at[look, p], near_send.at[at], near_recv.at[at], device(-1))

    def to_opp(p):
        return remote(own.at[sent_look, p], opp.at[p], opp_send.at[p], opp_recv.at[p], device(half))

    def to_far(p):
        return remote(own.at[0, p], far.at[p], far_send.at[p], far_recv.at[p], device(-2))

    def relay(p):
        sem = far_send.at[patches + p]
        return remote(near.at[0, p], far.at[p], sem, far_recv.at[p], device(-1))

    def to_hop(look, p):
        slot = look * (patches // 2) + p // 2
        return remote(own.at[look, p], hop.at[slot], hop_send.at[slot], hop_recv.at[slot], device(2))

    def onward_near(look, p):
        slot = look * (patches // 2) + p // 2
        at = look * patches + p
        return remote(hop.at[slot], near.at[look, p], onward_send.at[slot], near_recv.at[at], device(-3))

    def onward_far(p):
        slot = p // 2
        return remote(hop.at[slot], far.at[p], onward_send.at[slot], far_recv.at[p], device(-4))

    def forwarded_near(source, look):
        low_one = jnp.logical_and(source == 0, look == 1)
        return jnp.logical_or(low_one, jnp.logical_and(source == half, look == 0))

    def each_forward(p, act):
        at = forward_send.at[p]

        @pl.when(me == 0)
        def _():
            act(remote(opp.at[p], near.at[0, p], at, near_recv.at[p], device(half - 1)))

        @pl.when(me == 1)
        def _():
            act(remote(opp.at[p], far.at[p], at, far_recv.at[p], device(half - 2)))

        @pl.when(me == half)
        def _():
            act(remote(opp.at[p], near.at[1, p], at, near_recv.at[patches + p], device(half - 1)))

    def each_onward(act):
        for look in range(looks):
            for p in range(1, patches, 2):

                @pl.when(jnp.logical_not(jnp.logical_or(odd, forwarded_near(me - 2, look))))
                def _():
                    act(look, p, onward_near(look, p))

                if look == 0:

                    @pl.when(jnp.logical_and(odd, me != half + 3))
                    def _():
                        act(look, p, onward_far(p))

    def each_route(look, p, act):
        via = jnp.logical_and(crossing, p % 2 == 1)
        has_near = jnp.logical_not(forwarded_near(me, look))
        via_near = jnp.logical_and(jnp.logical_and(via, has_near), jnp.logical_not(odd))
        has_far = jnp.logical_and(jnp.logical_and(odd, look == 0), me != half + 1)
        via_far = jnp.logical_and(via, has_far)

        @pl.when(jnp.logical_or(via_near, via_far))
        def _():
            act(to_hop(look, p))

        @pl.when(jnp.logical_and(has_near, jnp.logical_not(via_near)))
        def _():
            act(to_near(look, p))

        @pl.when(jnp.logical_and(has_far, jnp.logical_not(via)))
        def _():
            act(to_far(p))

    def send(u):
        p = u % patches

        @pl.when(u < patches)
        def _():
            to_opp(p).start()

        @pl.when(u >= patches)
        def _():
            early = p < patches // 2
            look = jnp.where(early, sent_look, kept_look)
            for step in range(2):
                patch = 2 * lax.rem(p, patches // 2) + step
                each_route(look, patch, lambda copy: copy.start())

    for look in range(looks):
        energy[look] = jnp.zeros((8, 128), jnp.float32)

    def forward(u, carry):
        @pl.when(u > 0)
        def _():
            send(u - 1)

        look, p = look_at(u), u % patches
        load(u).wait()
        spec_even, spec_odd = spectrum_of(img.at[u], left_ref, right_ref)
        quarter = BAND // 2
        own[look, p, 0, :, :quarter] = spec_even[:, :quarter]
        own[look, p, 0, :, quarter:] = spec_odd[:, :quarter]
        own[look, p, 1, :, :quarter] = spec_even[:, quarter:]
        own[look, p, 1, :, quarter:] = spec_odd[:, quarter:]
        energy[look] += w_ref[p] * squares_of(spec_even, spec_odd)

        return carry

    tables[0].wait()
    tables[1].wait()
    lax.fori_loop(0, looks * patches, forward, 0)
    send(looks * patches - 1)

    tell = []
    for d, look_by in enumerate((0, 1, 2, half)):
        for by in range(nswath):
            if look_by or by:
                tell.append(remote(energy, heard.at[d, by], heard_send.at[d, by], heard_recv.at[d, by],
                                   device(-look_by, by)))
    for copy in tell:
        copy.start()

    rows = WIN // nswath
    mine = pl.ds(pl.multiple_of(lane * rows, rows), rows)

    def outgoing(slot, by):
        at = pl.ds(pl.multiple_of(lax.rem(lane + by, nswath) * rows, rows), rows)
        return remote(outbox.at[slot, at], inbox.at[by - 1, slot], box_send.at[by - 1, slot],
                      box_recv.at[by - 1, slot], device(0, by))

    def returned():
        return remote(turned, backbox, back_send.at[0], back_recv.at[0], device(half))

    def pair(slot, a, b_ref):
        cross_into(w_ref, own.at[a], b_ref, cre, cim)
        keep, turn = halves(first_ref, second_ref, cre, cim)
        value = keep - turn
        surf[slot] = value
        outbox[slot] = value.astype(jnp.bfloat16)
        both = slot is LAST
        if both:
            value = keep + turn
            surf[PAIRS] = value
            outbox[PAIRS] = value.astype(jnp.bfloat16)
        for by in range(1, nswath):
            if both:
                outgoing(PAIRS, by).start()
            outgoing(slot, by).start()

    tables[2].wait()
    tables[3].wait()
    pair(0, 0, own.at[1])

    @pl.when(jnp.logical_not(crossing))
    def _():
        def onward(look, p, copy):
            to_hop(look, p).wait_recv()
            copy.start()

        each_onward(onward)

    late = jnp.logical_and(odd, jnp.logical_not(crossing))

    def far_pair():
        for p in range(patches):
            to_far(p).wait_recv()
        pair(5, 1, far)

    def ring_pairs(with_far):
        ahead = lax.rem(me + 1, nlook)
        first_look = jnp.where(jnp.logical_and(ahead < half, ahead != 0), 1, 0)
        for look in (first_look, 1 - first_look):
            for p in range(patches):
                to_near(look, p).wait_recv()

                @pl.when(jnp.logical_and(odd, look == 0))
                def _():
                    relay(p).start()

            pair(1 + look, 0, near.at[look])
            pair(3 + look, 1, near.at[look])
            if with_far and look is first_look:
                far_pair()
    @pl.when(jnp.logical_not(late))
    def _():
        ring_pairs(False)

    for p in range(patches):
        to_opp(p).wait_recv()
        each_forward(p, lambda copy: copy.start())
    pair(LAST, kept_look, opp)

    for copy in tell:
        copy.wait_recv()
    total = []
    for d in range(4):
        for look in range(looks):
            parts = energy[look] if d == 0 else heard[d, 0, look]
            for by in range(1, nswath):
                parts = parts + heard[d, by, look]
            total.append(jnp.sum(parts, axis=(0, 1), keepdims=True))
    scale = BAND * math.sqrt(patches * nswath)

    def factor(look, lag):
        mate = total[look + lag + 1] if lag < 3 else total[3 * looks + look]
        return mask_ref[look, lag].astype(jnp.float32) * scale / jnp.sqrt(total[look] * mate)

    def summed(slot):
        value = surf[slot, mine, :]
        for by in range(1, nswath):
            outgoing(slot, by).wait_recv()
            value = value + inbox[by - 1, slot].astype(jnp.float32)
        return value

    def finish(slot):
        out_ref[slot // 3, slot % 3] = summed(slot)

    turned[...] = summed(PAIRS).astype(jnp.bfloat16)
    for look in range(looks):
        for lag in range(4):
            factor_ref[look, lag : lag + 1, :] = jnp.broadcast_to(factor(look, lag), (1, WIN))
    finish(0)
    returned().start()

    @pl.when(late)
    def _():
        ring_pairs(True)

    @pl.when(jnp.logical_not(late))
    def _():
        far_pair()

    finish(1)
    finish(3)
    kept = summed(PAIRS - 1)
    returned().wait_recv()
    back = backbox[...].astype(jnp.float32)
    out_ref[0, 3] = jnp.where(low, kept, back)
    out_ref[1, 3] = jnp.where(low, back, kept)
    finish(2)
    finish(4)
    finish(5)

    for look in range(looks):
        for p in range(patches):
            each_route(look, p, lambda copy: copy.wait_send())
    for p in range(patches):
        to_opp(p).wait_send()

        @pl.when(odd)
        def _():
            relay(p).wait_send()

        each_forward(p, lambda copy: copy.wait_send())

    @pl.when(jnp.logical_not(crossing))
    def _():
        each_onward(lambda look, p, copy: copy.wait_send())

    for copy in tell:
        copy.wait_send()
    returned().wait_send()
    for slot in range(PAIRS + 1):
        for by in range(1, nswath):
            outgoing(slot, by).wait_send()


def per_device(images, patch_weight, pair_mask):
    nlook = lax.axis_size("look")
    nswath = lax.axis_size("swath")
    looks, patches = images.shape[:2]
    left, right = forward_tables()
    first, second = inverse_tables()
    rows = WIN // nswath
    vmem = pl.BlockSpec(memory_space=pltpu.VMEM)
    smem = pl.BlockSpec(memory_space=pltpu.SMEM)
    dma = pltpu.SemaphoreType.DMA
    unit = (2, BAND, BAND)
    others = max(nswath - 1, 1)
    surfaces, factors = pl.pallas_call(
        functools.partial(kernel, nlook, nswath),
        in_specs=[smem, smem] + [pl.BlockSpec(memory_space=pltpu.HBM)] * 5,
        out_specs=[vmem, vmem],
        out_shape=[
            jax.ShapeDtypeStruct((looks, 4, rows, WIN), jnp.float32),
            jax.ShapeDtypeStruct((looks, 4, WIN), jnp.float32),
        ],
        scratch_shapes=[
            pltpu.VMEM(left.shape, jnp.bfloat16),
            pltpu.VMEM(right.shape, jnp.bfloat16),
            pltpu.VMEM(first.shape, jnp.bfloat16),
            pltpu.VMEM(second.shape, jnp.bfloat16),
            pltpu.VMEM((looks * patches, 2, PIX, PIX), jnp.bfloat16),
            pltpu.VMEM((looks * (patches // 2),) + unit, jnp.bfloat16),
            pltpu.VMEM((looks, patches) + unit, jnp.bfloat16),
            pltpu.VMEM((looks, patches) + unit, jnp.bfloat16),
            pltpu.VMEM((patches,) + unit, jnp.bfloat16),
            pltpu.VMEM((patches,) + unit, jnp.bfloat16),
            pltpu.VMEM((looks, 8, 128), jnp.float32),
            pltpu.VMEM((4, nswath, looks, 8, 128), jnp.float32),
            pltpu.VMEM((BAND, BAND), jnp.bfloat16),
            pltpu.VMEM((BAND, BAND), jnp.bfloat16),
            pltpu.VMEM((PAIRS + 1, WIN, WIN), jnp.float32),
            pltpu.VMEM((PAIRS + 1, WIN, WIN), jnp.bfloat16),
            pltpu.VMEM((others, PAIRS + 1, rows, WIN), jnp.bfloat16),
            pltpu.VMEM((rows, WIN), jnp.bfloat16),
            pltpu.VMEM((rows, WIN), jnp.bfloat16),
            dma((4,)),
            dma((looks * (patches // 2),)),
            dma((looks * (patches // 2),)),
            dma((looks * (patches // 2),)),
            dma((patches,)),
            dma((looks * patches,)),
            dma((looks * patches,)),
            dma((looks * patches,)),
            dma((2 * patches,)),
            dma((patches,)),
            dma((patches,)),
            dma((patches,)),
            dma((4, nswath)),
            dma((4, nswath)),
            dma((others, PAIRS + 1)),
            dma((others, PAIRS + 1)),
            dma((1,)),
            dma((1,)),
        ],
        compiler_params=pltpu.CompilerParams(
            collective_id=0, has_side_effects=True, vmem_limit_bytes=67043328
        ),
        name="autofocus",
    )(patch_weight, pair_mask, images, left, right, first, second)
    return surfaces * factors[:, :, None, :]


def solution(mesh):
    return jax.shard_map(
        per_device,
        mesh=mesh,
        in_specs=(P("look", "swath", None, None, None), P("swath"), P("look", None)),
        out_specs=P("look", None, "swath", None),
        check_vma=False,
    )
```
